32 devices in a mesh: mode: 8 (over z, x), space: 4 (over y, core).
Axes of the slice: x: 2, y: 2, z: 4, core: 2. Of those that a mesh axis runs over, the one named last changes fastest.
Arguments:
- forcing: float32 [64, 64, 256], P('mode', 'space'), may hold values from -8 to 8
- mean_field: float32 [64, 256], P('space'), may hold values from 0.5 to 2
- coef_fields: float32 [28, 64, 256], P(None, 'space'), may hold values from -3 to 3
- color: int32 [64], replicated, may hold values from 0 to 3, as said below
- pair_src: int32 [4, 64, 24], P(None, 'mode'), may hold values from 0 to 63, as said below
- pair_field: int32 [4, 64, 24], P(None, 'mode'), may hold values from 0 to 27
- pair_value: float32 [4, 64, 24], P(None, 'mode'), may hold values from -1.25 to 1.25
Outputs:
- solution: float32 [64, 64, 256], P('mode', 'space')
- residual: float32 [64, 64, 256], P('mode', 'space')
The draws below stay inside these ranges and needn't reach their ends.
Inputs may be any that keep to these rules, and one draw needn't show every extreme that they name: `color`: every aligned block of 8 modes holds exactly 2 modes of each batch. `pair_src`: the entries of batch c name only modes whose color is c.
All inputs are finite; a program needn't handle non-finite values.
Results may differ from the reference program's by a relative error of at most 0.0001.
Values sent between devices are 32-bit elements; how exact they have to be, the bound alone decides.
A program may use at most 64 MiB of HBM per device.

```python
import math
import jax
import jax.numpy as jnp
from jax import lax

NZ = 24
MODE_DEV = 8
NB = 4
SWEEPS = 2
K = 28
MODES = 64
NX = 64
NY = 256


def make_colors(key):
    blocks = MODES // MODE_DEV
    block_keys = jax.random.split(jax.random.fold_in(key, 11), blocks)
    orders = jax.vmap(lambda block_key: jax.random.permutation(block_key, MODE_DEV))(block_keys)
    return (orders % NB).reshape(-1).astype(jnp.int32)


def draw_color(key, part):
    return make_colors(key)


def draw_pair_src(key, part):
    colors = make_colors(key)
    blocks = MODES // MODE_DEV
    per_batch = MODE_DEV // NB
    grouped = colors.reshape(blocks, MODE_DEV)
    onehot = (grouped[:, :, None] == jnp.arange(NB, dtype=jnp.int32)[None, None, :]).astype(jnp.int32)
    earlier = jnp.cumsum(onehot, axis=1) - onehot
    ranking = jnp.sum(onehot * earlier, axis=2).reshape(-1)
    owners = jnp.arange(MODES, dtype=jnp.int32) // MODE_DEV
    lookup = jnp.zeros((blocks * NB * per_batch,), jnp.int32)
    lookup = lookup.at[owners * NB * per_batch + colors * per_batch + ranking].set(jnp.arange(MODES, dtype=jnp.int32))
    device_ids = jax.random.randint(jax.random.fold_in(key, 23), (NB, MODES, NZ), 0, blocks)
    slot_ids = jax.random.randint(jax.random.fold_in(key, 29), (NB, MODES, NZ), 0, per_batch)
    batch_ids = jnp.arange(NB, dtype=jnp.int32)[:, None, None]
    return jnp.take(lookup, device_ids * NB * per_batch + batch_ids * per_batch + slot_ids).astype(jnp.int32)


def set_ends(values, stream_key, smallest, high):
    longest = values.shape.index(max(values.shape))
    spots = []
    for shift in (0, 1):
        where = [jax.random.randint(jax.random.fold_in(stream_key, axis), (), 0, length) for axis, length in enumerate(values.shape)]
        where[longest] = (where[longest] + shift) % values.shape[longest]
        spots.append(tuple(where))
    return values.at[spots[0]].set(smallest).at[spots[1]].set(high)


def block_scale(rng, shape, pieces, least, largest):
    gain = 1.0
    for axis_at, blocks in pieces:
        draws = jax.random.uniform(jax.random.fold_in(jax.random.fold_in(rng, 6), axis_at), (blocks,), jnp.float32, least / len(pieces), largest / len(pieces))
        gain = gain * jnp.repeat(jnp.exp(draws), shape[axis_at] // blocks).reshape((-1,) + (1,) * (len(shape) - 1 - axis_at))
    return gain


def scatter_about(stream_key, extent, scale, most, pieces=(), held_as=jnp.bfloat16):
    level = block_scale(stream_key, extent, pieces, -0.22, 0.18) if pieces else 1.0
    array = jax.random.normal(stream_key, extent, jnp.float32) * scale * level
    return jnp.minimum(jnp.maximum(array, -most), most).astype(held_as)


def setup_inputs(seed: int = 0) -> dict:
    keys = jax.random.split(jax.random.key(seed), 8)
    forcing = scatter_about(keys[0], (MODES, NX, NY), 1.0, 8.0, ((0, 8), (1, 4)), jnp.float32)
    mean_field = jnp.clip(jnp.exp(math.log(2.0) - 1.3862944 * jax.random.uniform(keys[1], (NX, NY), jnp.float32) ** block_scale(keys[1], (NX, NY), ((0, 4),), -0.2, 0.2)), 0.5, 2.0)
    coef_fields = scatter_about(keys[2], (K, NX, NY), 0.5, 3.0, ((1, 4),), jnp.float32)
    color = draw_color(jax.random.fold_in(keys[7], 71), 0)
    pair_src = draw_pair_src(jax.random.fold_in(keys[7], 71), 0)
    pair_field = set_ends(jax.random.randint(keys[5], (NB, MODES, NZ), 0, K), jax.random.fold_in(keys[5], 1), 0, K - 1).astype(jnp.int32)
    pair_value = scatter_about(keys[6], (NB, MODES, NZ), NZ ** -0.5, 1.25, ((1, 8),), jnp.float32)
    return dict(forcing=forcing, mean_field=mean_field, coef_fields=coef_fields, color=color, pair_src=pair_src, pair_field=pair_field, pair_value=pair_value)


def stencil(coeff_field, values):
    height, breadth = coeff_field.shape
    coeff_pad = jnp.pad(coeff_field, ((1, 1), (1, 1)))
    value_pad = jnp.pad(values, ((1, 1), (1, 1)))
    result = jnp.zeros((height, breadth), jnp.float32)
    for step_x, step_y in ((1, 0), (-1, 0), (0, 1), (0, -1)):
        coeff_near = coeff_pad[1 + step_x:1 + step_x + height, 1 + step_y:1 + step_y + breadth]
        value_near = value_pad[1 + step_x:1 + step_x + height, 1 + step_y:1 + step_y + breadth]
        result = result + 0.5 * (coeff_field + coeff_near) * (values - value_near)
    return result


def face_sum(coeff_field):
    height, breadth = coeff_field.shape
    coeff_pad = jnp.pad(coeff_field, ((1, 1), (1, 1)))
    result = jnp.zeros((height, breadth), jnp.float32)
    for step_x, step_y in ((1, 0), (-1, 0), (0, 1), (0, -1)):
        coeff_near = coeff_pad[1 + step_x:1 + step_x + height, 1 + step_y:1 + step_y + breadth]
        result = result + 0.5 * (coeff_field + coeff_near)
    return result


def couple(update, sources, field_ids, weights, coef_fields):
    def reader(reader_entry):
        source_rows, field_rows, weight_rows = reader_entry
        values = jnp.take(update, source_rows, axis=0)
        coeffs = jnp.take(coef_fields, field_rows, axis=0)
        fluxes = jax.vmap(stencil)(coeffs, values)
        return jnp.sum(weight_rows[:, None, None] * fluxes, axis=0)
    return lax.map(reader, (sources, field_ids, weights))


def reference(forcing, mean_field, coef_fields, color, pair_src, pair_field, pair_value):
    diag_sum = face_sum(mean_field)
    solution = jnp.zeros(forcing.shape, jnp.float32)
    coupled = jnp.zeros(forcing.shape, jnp.float32)
    for sweep_idx in range(SWEEPS):
        for color_idx in range(NB):
            active = (color == color_idx)[:, None, None]
            update = jnp.where(active, (forcing - coupled) / diag_sum, 0.0)
            solution = solution + update
            coupled = coupled + couple(update, pair_src[color_idx], pair_field[color_idx], pair_value[color_idx], coef_fields)
    return solution, forcing - coupled
```

```python
import functools

import jax
import jax.numpy as jnp
from jax import lax
from jax.experimental import pallas as pl
from jax.experimental.pallas import tpu as pltpu
from jax.sharding import PartitionSpec as P

SWEEPS = 2
LANES = 128


def with_halo(block, sides, width):
    for axis, dim in sides:
        count = lax.axis_size(axis)
        forward = [(i, i + 1) for i in range(count - 1)]
        backward = [(target, source) for source, target in forward]
        low = lax.ppermute(
            lax.slice_in_dim(block, block.shape[dim] - width, None, axis=dim), axis, forward
        )
        high = lax.ppermute(lax.slice_in_dim(block, 0, width, axis=dim), axis, backward)
        block = jnp.concatenate([low, block, high], axis=dim)
    return block


def stencil_ext(coeff_ext, value_ext):
    coeff_mid = coeff_ext[1:-1]
    value_mid = value_ext[1:-1]
    coeff_side = jnp.pad(coeff_mid, ((0, 0), (1, 1)))
    value_side = jnp.pad(value_mid, ((0, 0), (1, 1)))
    result = 0.5 * (coeff_mid + coeff_ext[2:]) * (value_mid - value_ext[2:])
    result = result + 0.5 * (coeff_mid + coeff_ext[:-2]) * (value_mid - value_ext[:-2])
    result = result + 0.5 * (coeff_mid + coeff_side[:, 2:]) * (value_mid - value_side[:, 2:])
    result = result + 0.5 * (coeff_mid + coeff_side[:, :-2]) * (value_mid - value_side[:, :-2])
    return result


def face_sum_ext(coeff_ext):
    coeff_mid = coeff_ext[1:-1]
    coeff_side = jnp.pad(coeff_mid, ((0, 0), (1, 1)))
    result = 0.5 * (coeff_mid + coeff_ext[2:])
    result = result + 0.5 * (coeff_mid + coeff_ext[:-2])
    result = result + 0.5 * (coeff_mid + coeff_side[:, 2:])
    result = result + 0.5 * (coeff_mid + coeff_side[:, :-2])
    return result


def couple(gathered, sources, field_ids, weights, stacked_ext):

    def reader(reader_entry):
        source_rows, field_rows, weight_rows = reader_entry
        values = jnp.take(gathered, source_rows, axis=0)
        coeffs = jnp.take(stacked_ext, field_rows + 1, axis=0)
        fluxes = jax.vmap(stencil_ext)(coeffs, values)
        return jnp.sum(weight_rows[:, None, None] * fluxes, axis=0)

    return lax.map(reader, (sources, field_ids, weights))


def ranks(color, mode_dev, batches):
    grouped = color.reshape(-1, mode_dev)
    onehot = (grouped[:, :, None] == jnp.arange(batches, dtype=jnp.int32)[None, None, :]).astype(
        jnp.int32
    )
    earlier = jnp.cumsum(onehot, axis=1) - onehot
    return jnp.sum(onehot * earlier, axis=2).reshape(-1)


def by_batch(forcing, mean_field, coef_fields, color, pair_src, pair_field, pair_value):
    mode_dev = forcing.shape[0]
    batches = pair_src.shape[0]
    per_batch = mode_dev // batches
    stacked = jnp.concatenate([mean_field[None], coef_fields], axis=0)
    stacked_ext = with_halo(stacked, (("space", 1),), 1)
    diag_sum = face_sum_ext(stacked_ext[0])
    ranking = ranks(color, mode_dev, batches)
    owners = jnp.arange(color.shape[0], dtype=jnp.int32) // mode_dev
    pool_rows = owners * per_batch + ranking
    source_rows = jnp.take(pool_rows, pair_src, axis=0)
    offset = lax.axis_index("mode") * mode_dev
    local_color = lax.dynamic_slice_in_dim(color, offset, mode_dev)
    local_rank = lax.dynamic_slice_in_dim(ranking, offset, mode_dev)
    positions = jnp.arange(mode_dev, dtype=jnp.int32)
    slot_numbers = jnp.arange(per_batch, dtype=jnp.int32)
    solution = jnp.zeros(forcing.shape, jnp.float32)
    coupled = jnp.zeros(forcing.shape, jnp.float32)
    for sweep_idx in range(SWEEPS):
        for color_idx in range(batches):
            active = local_color == color_idx
            update = jnp.where(active[:, None, None], (forcing - coupled) / diag_sum, 0.0)
            solution = solution + update
            selected = (active[None, :] & (local_rank[None, :] == slot_numbers[:, None])).astype(
                jnp.int32
            )
            chosen = jnp.sum(positions[None, :] * selected, axis=1)
            own_update = jnp.take(update, chosen, axis=0)
            inner = lax.all_gather(own_update, "mode", axis=0, tiled=True)
            gathered = with_halo(inner, (("space", 1),), 1)
            coupled = coupled + couple(
                gathered,
                source_rows[color_idx],
                pair_field[color_idx],
                pair_value[color_idx],
                stacked_ext,
            )
    return (solution, forcing - coupled)


def sweep_kernel(dims, color, psrc, pfield, pval, forcing, mean, coef, sol_out, res_out,
                 shade, src_v, field_v, val_v, force_v, mean_v, ext, outs, msg, allp, win, land, cbuf, ax, ay,
                 inv, w2, r, sol, dvx, dvy, spack, rpack, back, local, send, recv, hsend, hrecv,
                 csend, crecv):
    batches, sources, modes, width, steps, cells, rows, fields, nz, owners, slabs = dims
    mode_dev = modes // owners
    per_batch = mode_dev // batches
    edge = width * steps
    core_cells = cells - 2 * edge
    slab_rows = core_cells // width
    cols = width - 2 * steps
    ny = cols * owners
    me = lax.axis_index("mode")
    slab = lax.axis_index("space")
    low, mid_at, high = pl.ds(0, edge), pl.ds(edge, core_cells), pl.ds(cells - edge, edge)
    has_low, has_high = slab > 0, slab < slabs - 1

    def peer(d):
        return lax.rem(me + d, owners)

    def origin(d):
        return lax.rem(me + owners - d, owners)

    barrier = pltpu.get_barrier_semaphore()
    for d in range(1, owners):
        pl.semaphore_signal(
            barrier, inc=1, device_id={"mode": peer(d)}, device_id_type=pl.DeviceIdType.MESH
        )
    for there, at in ((has_low, slab - 1), (has_high, slab + 1)):

        @pl.when(there)
        def _():
            pl.semaphore_signal(
                barrier, inc=1, device_id={"space": at}, device_id_type=pl.DeviceIdType.MESH
            )

    def remote(src, dst, ssem, rsem, **where):
        return pltpu.make_async_remote_copy(
            src_ref=src, dst_ref=dst, send_sem=ssem, recv_sem=rsem, device_id=where,
            device_id_type=pl.DeviceIdType.MESH,
        )

    def pair_copy(d, o):
        return remote(msg, allp.at[o], send.at[0, d], recv.at[0, d], mode=peer(d))

    def value_copy(c, d, o):
        return remote(
            win.at[peer(d), c], land.at[c, o, :, mid_at], send.at[1 + c, d], recv.at[1 + c, d],
            mode=peer(d),
        )

    def up_copy(c):
        return remote(
            land.at[c, :, :, pl.ds(core_cells, edge)], land.at[c, :, :, low],
            hsend.at[0, c], hrecv.at[0, c], space=slab + 1,
        )

    def down_copy(c):
        return remote(
            land.at[c, :, :, pl.ds(edge, edge)], land.at[c, :, :, high],
            hsend.at[1, c], hrecv.at[1, c], space=slab - 1,
        )

    def coef_up():
        return remote(
            cbuf.at[:, pl.ds(core_cells, edge)], cbuf.at[:, low], csend.at[0], crecv.at[0],
            space=slab + 1,
        )

    def coef_down():
        return remote(
            cbuf.at[:, pl.ds(edge, edge)], cbuf.at[:, high], csend.at[1], crecv.at[1],
            space=slab - 1,
        )

    def solution_copy(c, d):
        return remote(
            spack.at[c, peer(d)], back.at[0, me, c], send.at[1 + batches + c, d],
            recv.at[1 + batches + c, d], mode=peer(d),
        )

    def residual_copy(d):
        return remote(
            rpack.at[peer(d)], back.at[1, me], send.at[1 + 2 * batches, d],
            recv.at[1 + 2 * batches, d], mode=peer(d),
        )

    loads = [
        pltpu.make_async_copy(src, dst, local.at[n])
        for n, (src, dst) in enumerate(
            (
                (color, shade), (psrc, src_v), (pfield, field_v), (pval, val_v),
                (forcing, force_v), (mean, mean_v),
            )
        )
    ]
    halves = ny // LANES
    for h in range(halves):
        part = pl.ds(h * LANES, LANES)
        loads.append(
            pltpu.make_async_copy(
                coef.at[:, part], ext.at[h, pl.ds(0, fields * slab_rows)], local.at[6 + h]
            )
        )
    for one in loads:
        one.start()

    for there, at in ((has_low, low), (has_high, high)):

        @pl.when(jnp.logical_not(there))
        def _():
            for c in range(batches):
                land[c, :, :, at] = jnp.zeros((owners, per_batch, edge), jnp.float32)
            cbuf[:, at] = jnp.zeros((cbuf.shape[0], edge), jnp.float32)

    r[...] = jnp.zeros_like(r)

    def earlier(shades, j):
        found = jnp.int32(0)
        for i in range(j):
            found = found | (shades[i] == shades[j]).astype(jnp.int32)
        return found

    loads[0].wait()
    second = []
    for o in range(owners):
        shades = [shade[o * mode_dev + j] for j in range(mode_dev)]
        second.append(
            functools.reduce(
                lambda x, y: x | y, [earlier(shades, j) << j for j in range(1, mode_dev)]
            )
        )
    shades = [shade[me * mode_dev + j] for j in range(mode_dev)]
    slots = [shades[j] * per_batch + earlier(shades, j) for j in range(mode_dev)]
    sub = lax.broadcasted_iota(jnp.int32, (mode_dev, ny), 0)
    holds = [sub == slots[j] for j in range(mode_dev)]

    def choose(masks, lines, shape):
        out = jnp.broadcast_to(lines[0], shape)
        for j in range(1, mode_dev):
            out = jnp.where(masks[j], jnp.broadcast_to(lines[j], shape), out)
        return out

    for n in (1, 2, 3):
        loads[n].wait()
    keys, vals = [], []
    for c in range(batches):
        src = src_v[c]
        owner = src >> 3
        bits = jnp.zeros_like(src)
        for o in range(owners):
            bits = jnp.where(owner == o, second[o], bits)
        source = owner * per_batch + ((bits >> (src & 7)) & 1)
        keys.append((field_v[c] * sources + source).astype(jnp.float32))
        vals.append(val_v[c])
    rest = jnp.zeros((mode_dev, LANES - batches * nz), jnp.float32)
    both = jnp.concatenate(keys + [rest] + vals + [rest], axis=1)
    lanes2 = 2 * LANES
    both = choose(
        [m[:, :lanes2] for m in holds], [both[j : j + 1] for j in range(mode_dev)],
        (mode_dev, lanes2),
    )
    for c in range(batches):
        msg[c] = both[c * per_batch : (c + 1) * per_batch]
        allp[me, c] = both[c * per_batch : (c + 1) * per_batch]

    loads[4].wait()
    lines = []
    for n in range(slab_rows):
        lines.append(
            choose(
                holds, [force_v[pl.ds(j * slab_rows + n, 1), :] for j in range(mode_dev)],
                (mode_dev, ny),
            )
        )
    blank = jnp.zeros((mode_dev, steps), jnp.float32)
    for p in range(owners):
        start, stop = p * cols - steps, (p + 1) * cols + steps
        parts = []
        for line in lines:
            if start < 0:
                parts.append(blank)
            parts.append(line[:, max(start, 0) : min(stop, ny)])
            if stop > ny:
                parts.append(blank)
        flat = jnp.concatenate(parts, axis=1)
        for c in range(batches):
            win[p, c] = flat[c * per_batch : (c + 1) * per_batch]

    beside = has_low.astype(jnp.int32) + has_high.astype(jnp.int32)
    pl.semaphore_wait(barrier, owners - 1 + beside)
    for d in range(1, owners):
        pair_copy(d, me).start()
    for c in range(batches):
        for d in range(1, owners):
            value_copy(c, d, me).start()
    for c in range(batches):
        land[c, me, :, mid_at] = win[me, c]

    loads[5].wait()
    m = mean_v[...]
    place = lax.broadcasted_iota(jnp.int32, (slab_rows, ny), 1)
    level = lax.broadcasted_iota(jnp.int32, (slab_rows, ny), 0)
    right = jnp.where(place < ny - 1, pltpu.roll(m, ny - 1, 1), 0.0)
    left = jnp.where(place > 0, pltpu.roll(m, 1, 1), 0.0)
    after = jnp.where(level < slab_rows - 1, pltpu.roll(m, slab_rows - 1, 0), 0.0)
    before = jnp.where(level > 0, pltpu.roll(m, 1, 0), 0.0)
    for n, x in enumerate((m, 4.0 * m + right + left, before, after)):
        for h in range(halves):
            ext[h, pl.ds((fields + n) * slab_rows, slab_rows), :] = x[:, h * LANES : (h + 1) * LANES]
    for h in range(halves):
        loads[6 + h].wait()
    kpad = cbuf.shape[0]
    shift = lax.rem(ny - (me * cols - steps), ny)
    column = lax.broadcasted_iota(jnp.int32, (kpad, width), 1) + (me * cols - steps)
    real = (column >= 0) & (column < ny)
    parts = []
    for n in range(slab_rows):
        x = jnp.concatenate(
            [ext[h, pl.ds(n, kpad, stride=slab_rows), :] for h in range(halves)], axis=1
        )
        x = pltpu.roll(x, shift, 1)
        parts.append(jnp.where(real, x[:, :width], 0.0))
    cbuf[:, mid_at] = jnp.concatenate(parts, axis=1)
    pl.when(has_high)(lambda: coef_up().start())
    pl.when(has_low)(lambda: coef_down().start())

    for d in range(1, owners):
        pair_copy(d, me).wait_recv()
    lane_f = lax.broadcasted_iota(jnp.int32, (8, LANES), 1).astype(jnp.float32)
    spread = w2.shape[2] // LANES
    per_tile = 8 // per_batch

    def fill(c, half, n):
        own = allp[pl.ds(half * per_tile, per_tile), n].reshape(8, 2 * LANES)
        sums = [jnp.zeros((8, LANES), jnp.float32)] * spread
        for z in range(nz):
            e = c * nz + z
            key = jnp.broadcast_to(own[:, e : e + 1], (8, LANES))
            val = jnp.broadcast_to(own[:, LANES + e : LANES + e + 1], (8, LANES))
            for g in range(spread):
                sums[g] = sums[g] + jnp.where(key == lane_f + float(g * LANES), val, 0.0)
        return jnp.concatenate(sums, axis=1)

    for c in range(batches):
        for n in range(batches):
            full = jnp.concatenate([fill(c, half, n) for half in range(owners // per_tile)], axis=0)
            hi = full.astype(jnp.bfloat16)
            w2[c, pl.ds(n * sources, sources), :] = hi
            w2[c, pl.ds(modes + n * sources, sources), :] = (
                full - hi.astype(jnp.float32)
            ).astype(jnp.bfloat16)

    def forward(c):
        for d in range(1, owners):
            value_copy(c, d, me).wait_recv()
        pl.when(has_high)(lambda: up_copy(c).start())
        pl.when(has_low)(lambda: down_copy(c).start())

    forward(0)
    pl.when(has_low)(lambda: coef_up().wait_recv())
    pl.when(has_high)(lambda: coef_down().wait_recv())
    a = cbuf[...]
    ax[...] = 0.5 * (a + pltpu.roll(a, cells - width, 1))
    ay[...] = 0.5 * (a + pltpu.roll(a, cells - 1, 1))
    centre, across = a[fields : fields + 1], a[fields + 1 : fields + 2]
    place = lax.broadcasted_iota(jnp.int32, (1, cells), 1)
    above = jnp.where(place < width, a[fields + 2 : fields + 3], pltpu.roll(centre, width, 1))
    below = jnp.where(
        place >= width * (rows - 1), a[fields + 3 : fields + 4],
        pltpu.roll(centre, cells - width, 1),
    )
    inside = across > 0.0
    diag = jnp.where(inside, 0.5 * (across + above + below), 1.0)
    inv[...] = jnp.where(inside, 1.0 / diag, 0.0)
    forward(1)
    forward(2)

    def compact(x):
        return jnp.concatenate(
            [x[:, q * width + steps : q * width + steps + cols] for q in range(slab_rows)], axis=1
        )

    def unfold(x, n):
        return [x[o * per_batch : (o + 1) * per_batch] for o in range(n)]

    for k in range(steps):
        c = k % batches
        first = (width * k) // LANES
        last = -(-(width * (rows - 1 - k)) // LANES)
        reach = -(-(width * (rows - k)) // LANES)
        size = (reach - first) * LANES
        span = pl.ds(first * LANES, size)
        mine = pl.ds(c * sources, sources)
        if k < batches:
            if k == 1:
                forward(3)
            pl.when(has_low)(lambda: up_copy(c).wait_recv())
            pl.when(has_high)(lambda: down_copy(c).wait_recv())
            r[mine, :] = r[mine, :] + land[c].reshape(sources, cells)
        u = r[mine, span] * inv[:, span]
        dvx[:, span] = u - pltpu.roll(u, size - width, 1)
        dvy[:, span] = u - pltpu.roll(u, size - 1, 1)
        inner = u[:, edge - first * LANES : edge - first * LANES + core_cells]
        if k < batches:
            sol[mine, :] = inner
        else:
            done = compact(sol[mine, :] + inner)
            for o in range(owners):
                spack[c, o] = done[o * per_batch : (o + 1) * per_batch]
            for d in range(1, owners):
                solution_copy(c, d).start()
            back[0, me, c] = spack[c, me]

        def flux(table, diff, at, w):
            his, mids = [], []
            d = diff[:, at]
            for f in range(fields):
                p = jnp.broadcast_to(table[pl.ds(f, 1), at], (sources, w)) * d
                hi = p.astype(jnp.bfloat16)
                his.append(hi)
                mids.append((p - hi.astype(jnp.float32)).astype(jnp.bfloat16))
            depth = fields * sources
            got = jnp.dot(
                w2[c, :, pl.ds(0, depth)], jnp.concatenate(his, axis=0),
                preferred_element_type=jnp.float32,
            )
            more = jnp.dot(
                w2[c, pl.ds(0, modes), pl.ds(0, depth)], jnp.concatenate(mids, axis=0),
                preferred_element_type=jnp.float32,
            )
            return got[:modes] + got[modes:] + more

        before = [None, None]
        for g in range(first, last, 2):
            w = LANES * min(2, last - g)
            at = pl.ds(g * LANES, w)
            lane = lax.broadcasted_iota(jnp.int32, (modes, w), 1)
            div = None
            for n, (table, diff, hop) in enumerate(((ax, dvx, width), (ay, dvy, 1))):
                x = flux(table, diff, at, w)
                turned = pltpu.roll(x, hop, 1)
                if before[n] is None:
                    shifted = turned
                else:
                    shifted = jnp.where(lane < hop, before[n][:, :w], turned)
                before[n] = turned
                div = x - shifted if div is None else div + (x - shifted)
            r[:, at] = r[:, at] - div

    done = jnp.concatenate(
        [compact(r[pl.ds(n * 8, 8), mid_at]) for n in range(modes // 8)], axis=0
    )
    for n in range(batches):
        for o in range(owners):
            at = n * sources + o * per_batch
            rpack[o, n] = done[at : at + per_batch]
    for d in range(1, owners):
        residual_copy(d).start()
    back[1, me] = rpack[me]

    row_slot = jnp.zeros((mode_dev, ny), jnp.int32)
    for j in range(mode_dev):
        row_slot = jnp.where(sub == j, slots[j], row_slot)
    gives = [row_slot == s for s in range(mode_dev)]

    def out_copy(which, h):
        return pltpu.make_async_copy(
            outs.at[which, h], (sol_out, res_out)[which].at[:, pl.ds(h * LANES, LANES)],
            local.at[8 + 2 * which + h],
        )

    def restore(which):
        got = [back[which, p].reshape(mode_dev, slab_rows * cols) for p in range(owners)]
        for n in range(slab_rows):
            line = jnp.concatenate([x[:, n * cols : (n + 1) * cols] for x in got], axis=1)
            line = choose(gives, [line[s : s + 1] for s in range(mode_dev)], (mode_dev, ny))
            for h in range(halves):
                outs[which, h, pl.ds(n, mode_dev, stride=slab_rows), :] = line[
                    :, h * LANES : (h + 1) * LANES
                ]
        for h in range(halves):
            out_copy(which, h).start()

    for d in range(1, owners):
        pair_copy(d, me).wait_send()
        for c in range(batches):
            value_copy(c, d, me).wait_send()
    for c in range(batches):
        pl.when(has_high)(lambda: up_copy(c).wait_send())
        pl.when(has_low)(lambda: down_copy(c).wait_send())
    pl.when(has_high)(lambda: coef_up().wait_send())
    pl.when(has_low)(lambda: coef_down().wait_send())
    for d in range(1, owners):
        for c in range(batches):
            solution_copy(c, d).wait_send()
            solution_copy(c, d).wait_recv()
    restore(0)
    for d in range(1, owners):
        residual_copy(d).wait_send()
        residual_copy(d).wait_recv()
    restore(1)
    for which in range(2):
        for h in range(halves):
            out_copy(which, h).wait()


def patch_sizes(mesh, forcing, pair_src, coef_fields):
    owners = mesh.shape["mode"]
    slabs = mesh.shape["space"]
    modes, nx, ny = forcing.shape
    batches = pair_src.shape[0]
    nz = pair_src.shape[2]
    fields = coef_fields.shape[0]
    depth = SWEEPS * batches
    slab = nx // slabs
    cols = ny // owners
    width = cols + 2 * depth
    rows = slab + 2 * depth
    cells = rows * width
    sources = modes // batches
    fits = (
        slab > depth
        and cells % (2 * LANES) == 0
        and (slab * cols) % LANES == 0
        and (width * depth) % LANES == 0
        and width <= LANES
        and modes == 8 * owners
        and owners == 8
        and batches == 4
        and sources == 16
        and slab % 8 == 0
        and ny == 2 * LANES
        and fields <= 28
        and batches * nz <= LANES
    )
    return fits, (batches, sources, modes, width, depth, cells, rows, fields, nz, owners, slabs)


def by_patch(dims, forcing, mean_field, coef_fields, color, pair_src, pair_field, pair_value):
    batches, sources, modes, width, depth, cells, rows, fields, nz, owners, slabs = dims
    mode_dev, slab, ny = forcing.shape
    per_batch = mode_dev // batches
    cols = ny // owners
    core_cells = slab * width
    kpad = 32
    spread = -(-(fields * sources) // LANES) * LANES

    anywhere = pl.BlockSpec(memory_space=pl.ANY)
    f32, i32 = jnp.float32, jnp.int32
    flat = jax.ShapeDtypeStruct((mode_dev * slab, ny), f32)
    sems = pltpu.SemaphoreType.DMA
    got = pl.pallas_call(
        functools.partial(sweep_kernel, dims),
        out_shape=(flat, flat),
        in_specs=[anywhere] * 7,
        out_specs=(anywhere, anywhere),
        scratch_shapes=[
            pltpu.SMEM((modes,), i32),
            pltpu.VMEM((batches, mode_dev, nz), i32),
            pltpu.VMEM((batches, mode_dev, nz), i32),
            pltpu.VMEM((batches, mode_dev, nz), f32),
            pltpu.VMEM((mode_dev * slab, ny), f32),
            pltpu.VMEM((slab, ny), f32),
            pltpu.VMEM((ny // LANES, kpad * slab, LANES), f32),
            pltpu.VMEM((2, ny // LANES, mode_dev * slab, LANES), f32),
            pltpu.VMEM((batches, per_batch, 2 * LANES), f32),
            pltpu.VMEM((owners, batches, per_batch, 2 * LANES), f32),
            pltpu.VMEM((owners, batches, per_batch, core_cells), f32),
            pltpu.VMEM((batches, owners, per_batch, cells), f32),
            pltpu.VMEM((kpad, cells), f32),
            pltpu.VMEM((kpad, cells), f32),
            pltpu.VMEM((kpad, cells), f32),
            pltpu.VMEM((1, cells), f32),
            pltpu.VMEM((batches, 2 * modes, spread), jnp.bfloat16),
            pltpu.VMEM((modes, cells), f32),
            pltpu.VMEM((modes, core_cells), f32),
            pltpu.VMEM((sources, cells), f32),
            pltpu.VMEM((sources, cells), f32),
            pltpu.VMEM((batches, owners, per_batch, slab * cols), f32),
            pltpu.VMEM((owners, batches, per_batch, slab * cols), f32),
            pltpu.VMEM((2, owners, batches, per_batch, slab * cols), f32),
            sems((12,)),
            sems((2 + 2 * batches, owners)),
            sems((2 + 2 * batches, owners)),
            sems((2, batches)),
            sems((2, batches)),
            sems((2,)),
            sems((2,)),
        ],
        compiler_params=pltpu.CompilerParams(collective_id=0, has_side_effects=True),
        name="sweeps",
    )(
        color, pair_src, pair_field, pair_value, forcing.reshape(mode_dev * slab, ny), mean_field,
        coef_fields.reshape(fields * slab, ny),
    )
    return tuple(x.reshape(mode_dev, slab, ny) for x in got)


def solution(mesh):
    specs = (
        P("mode", "space", None),
        P("space", None),
        P(None, "space", None),
        P(),
        P(None, "mode", None),
        P(None, "mode", None),
        P(None, "mode", None),
    )

    def whole(*args):
        fits, dims = patch_sizes(mesh, args[0], args[4], args[2])
        body = functools.partial(by_patch, dims) if fits else by_batch
        return jax.shard_map(
            body,
            mesh=mesh,
            in_specs=specs,
            out_specs=(P("mode", "space", None), P("mode", "space", None)),
            check_vma=False,
        )(*args)

    return whole
```

```python
import functools

import jax
import jax.numpy as jnp
from jax import lax
from jax.experimental import pallas as pl
from jax.experimental.pallas import tpu as pltpu
from jax.sharding import PartitionSpec as P

SWEEPS = 2
LANES = 128
PIECES = 2
WIDE = 2


def with_halo(block, sides, width):
    for axis, dim in sides:
        count = lax.axis_size(axis)
        forward = [(i, i + 1) for i in range(count - 1)]
        backward = [(target, source) for source, target in forward]
        low = lax.ppermute(
            lax.slice_in_dim(block, block.shape[dim] - width, None, axis=dim), axis, forward
        )
        high = lax.ppermute(lax.slice_in_dim(block, 0, width, axis=dim), axis, backward)
        block = jnp.concatenate([low, block, high], axis=dim)
    return block


def stencil_ext(coeff_ext, value_ext):
    coeff_mid = coeff_ext[1:-1]
    value_mid = value_ext[1:-1]
    coeff_side = jnp.pad(coeff_mid, ((0, 0), (1, 1)))
    value_side = jnp.pad(value_mid, ((0, 0), (1, 1)))
    result = 0.5 * (coeff_mid + coeff_ext[2:]) * (value_mid - value_ext[2:])
    result = result + 0.5 * (coeff_mid + coeff_ext[:-2]) * (value_mid - value_ext[:-2])
    result = result + 0.5 * (coeff_mid + coeff_side[:, 2:]) * (value_mid - value_side[:, 2:])
    result = result + 0.5 * (coeff_mid + coeff_side[:, :-2]) * (value_mid - value_side[:, :-2])
    return result


def face_sum_ext(coeff_ext):
    coeff_mid = coeff_ext[1:-1]
    coeff_side = jnp.pad(coeff_mid, ((0, 0), (1, 1)))
    result = 0.5 * (coeff_mid + coeff_ext[2:])
    result = result + 0.5 * (coeff_mid + coeff_ext[:-2])
    result = result + 0.5 * (coeff_mid + coeff_side[:, 2:])
    result = result + 0.5 * (coeff_mid + coeff_side[:, :-2])
    return result


def couple(gathered, sources, field_ids, weights, stacked_ext):

    def reader(reader_entry):
        source_rows, field_rows, weight_rows = reader_entry
        values = jnp.take(gathered, source_rows, axis=0)
        coeffs = jnp.take(stacked_ext, field_rows + 1, axis=0)
        fluxes = jax.vmap(stencil_ext)(coeffs, values)
        return jnp.sum(weight_rows[:, None, None] * fluxes, axis=0)

    return lax.map(reader, (sources, field_ids, weights))


def ranks(color, mode_dev, batches):
    grouped = color.reshape(-1, mode_dev)
    onehot = (grouped[:, :, None] == jnp.arange(batches, dtype=jnp.int32)[None, None, :]).astype(
        jnp.int32
    )
    earlier = jnp.cumsum(onehot, axis=1) - onehot
    return jnp.sum(onehot * earlier, axis=2).reshape(-1)


def by_batch(forcing, mean_field, coef_fields, color, pair_src, pair_field, pair_value):
    mode_dev = forcing.shape[0]
    batches = pair_src.shape[0]
    per_batch = mode_dev // batches
    stacked = jnp.concatenate([mean_field[None], coef_fields], axis=0)
    stacked_ext = with_halo(stacked, (("space", 1),), 1)
    diag_sum = face_sum_ext(stacked_ext[0])
    ranking = ranks(color, mode_dev, batches)
    owners = jnp.arange(color.shape[0], dtype=jnp.int32) // mode_dev
    pool_rows = owners * per_batch + ranking
    source_rows = jnp.take(pool_rows, pair_src, axis=0)
    offset = lax.axis_index("mode") * mode_dev
    local_color = lax.dynamic_slice_in_dim(color, offset, mode_dev)
    local_rank = lax.dynamic_slice_in_dim(ranking, offset, mode_dev)
    positions = jnp.arange(mode_dev, dtype=jnp.int32)
    slot_numbers = jnp.arange(per_batch, dtype=jnp.int32)
    solution = jnp.zeros(forcing.shape, jnp.float32)
    coupled = jnp.zeros(forcing.shape, jnp.float32)
    for sweep_idx in range(SWEEPS):
        for color_idx in range(batches):
            active = local_color == color_idx
            update = jnp.where(active[:, None, None], (forcing - coupled) / diag_sum, 0.0)
            solution = solution + update
            selected = (active[None, :] & (local_rank[None, :] == slot_numbers[:, None])).astype(
                jnp.int32
            )
            chosen = jnp.sum(positions[None, :] * selected, axis=1)
            own_update = jnp.take(update, chosen, axis=0)
            inner = lax.all_gather(own_update, "mode", axis=0, tiled=True)
            gathered = with_halo(inner, (("space", 1),), 1)
            coupled = coupled + couple(
                gathered,
                source_rows[color_idx],
                pair_field[color_idx],
                pair_value[color_idx],
                stacked_ext,
            )
    return (solution, forcing - coupled)


def sweep_kernel(dims, color, psrc, pfield, pval, forcing, mean, coef, outs, sides,
                 turn, shade, src_v, field_v, val_v, force_v, mean_v, ext, msg, allp, win, land, cbuf, faces,
                 inv, w2, r, sol, ready, diffs, spack, rpack, back, tail, local, send, recv, hsend, hrecv,
                 csend, crecv):
    batches, sources, modes, width, steps, cells, rows, fields, nz, owners, slabs = dims
    mode_dev = modes // owners
    per_batch = mode_dev // batches
    edge = width * steps
    core_cells = cells - 2 * edge
    slab_rows = core_cells // width
    cols = width - 2 * steps
    ny = cols * owners
    me = lax.axis_index("mode")
    slab = lax.axis_index("space")
    low, mid_at, high = pl.ds(0, edge), pl.ds(edge, core_cells), pl.ds(cells - edge, edge)
    has_low, has_high = slab > 0, slab < slabs - 1

    def peer(d):
        at = me
        bit = 1
        while bit < owners:
            if d & bit:
                at = at + bit * (1 - 2 * (me // bit % 2))
            bit *= 2
        return at

    far = range(owners - 1, 0, -1)

    barrier = pltpu.get_barrier_semaphore()
    for d in far:
        pl.semaphore_signal(
            barrier, inc=1, device_id={"mode": peer(d)}, device_id_type=pl.DeviceIdType.MESH
        )
    for there, at in ((has_low, slab - 1), (has_high, slab + 1)):

        @pl.when(there)
        def _():
            pl.semaphore_signal(
                barrier, inc=1, device_id={"space": at}, device_id_type=pl.DeviceIdType.MESH
            )

    def remote(src, dst, ssem, rsem, **where):
        return pltpu.make_async_remote_copy(
            src_ref=src, dst_ref=dst, send_sem=ssem, recv_sem=rsem, device_id=where,
            device_id_type=pl.DeviceIdType.MESH,
        )

    def pair_copy(d):
        return remote(msg, allp.at[me], send.at[0, d], recv.at[0, d], mode=peer(d))

    def value_copy(c, d):
        return remote(
            win.at[peer(d), c], land.at[c, me, :, mid_at], send.at[1 + c, d], recv.at[1 + c, d],
            mode=peer(d),
        )

    def up_copy(c):
        return remote(
            land.at[c, :, :, pl.ds(core_cells, edge)], land.at[c, :, :, low],
            hsend.at[0, c], hrecv.at[0, c], space=slab + 1,
        )

    def down_copy(c):
        return remote(
            land.at[c, :, :, pl.ds(edge, edge)], land.at[c, :, :, high],
            hsend.at[1, c], hrecv.at[1, c], space=slab - 1,
        )

    def coef_up():
        return remote(
            cbuf.at[:, pl.ds(core_cells, edge)], cbuf.at[:, low], csend.at[0], crecv.at[0],
            space=slab + 1,
        )

    def coef_down():
        return remote(
            cbuf.at[:, pl.ds(edge, edge)], cbuf.at[:, high], csend.at[1], crecv.at[1],
            space=slab - 1,
        )

    def solution_copy(c, d):
        return remote(
            spack.at[c, peer(d)], back.at[c, me], send.at[1 + batches + c, d],
            recv.at[1 + batches + c, d], mode=peer(d),
        )

    def residual_copy(n, d):
        return remote(
            rpack.at[n, peer(d)], tail.at[n, me], send.at[1 + 2 * batches + n, d],
            recv.at[1 + 2 * batches + n, d], mode=peer(d),
        )

    loads = [
        pltpu.make_async_copy(src, dst, local.at[n])
        for n, (src, dst) in enumerate(
            (
                (color, shade), (psrc, src_v), (pfield, field_v), (pval, val_v),
                (forcing, force_v), (mean, mean_v),
            )
        )
    ]
    halves = ny // LANES
    for h in range(halves):
        part = pl.ds(h * LANES, LANES)
        loads.append(
            pltpu.make_async_copy(
                coef.at[:, part], ext.at[h, pl.ds(0, fields * slab_rows)], local.at[6 + h]
            )
        )
    for one in loads:
        one.start()

    for there, at in ((has_low, low), (has_high, high)):

        @pl.when(jnp.logical_not(there))
        def _():
            for c in range(batches):
                land[c, :, :, at] = jnp.zeros((owners, per_batch, edge), jnp.float32)
            cbuf[:, at] = jnp.zeros((cbuf.shape[0], edge), jnp.float32)

    r[...] = jnp.zeros_like(r)

    def earlier(shades, j):
        found = jnp.int32(0)
        for i in range(j):
            found = found | (shades[i] == shades[j]).astype(jnp.int32)
        return found

    loads[0].wait()
    second = []
    for o in range(owners):
        shades = [shade[o * mode_dev + j] for j in range(mode_dev)]
        second.append(
            functools.reduce(
                lambda x, y: x | y, [earlier(shades, j) << j for j in range(1, mode_dev)]
            )
        )
    shades = [shade[me * mode_dev + j] for j in range(mode_dev)]
    slots = [shades[j] * per_batch + earlier(shades, j) for j in range(mode_dev)]
    sub = lax.broadcasted_iota(jnp.int32, (mode_dev, ny), 0)
    holds = [sub == slots[j] for j in range(mode_dev)]

    def choose(masks, lines, shape):
        out = jnp.broadcast_to(lines[0], shape)
        for j in range(1, mode_dev):
            out = jnp.where(masks[j], jnp.broadcast_to(lines[j], shape), out)
        return out

    for n in (1, 2, 3):
        loads[n].wait()
    keys, vals = [], []
    for c in range(batches):
        src = src_v[c]
        owner = src >> 3
        bits = jnp.zeros_like(src)
        for o in range(owners):
            bits = jnp.where(owner == o, second[o], bits)
        source = owner * per_batch + ((bits >> (src & 7)) & 1)
        keys.append((field_v[c] * sources + source).astype(jnp.float32))
        vals.append(val_v[c])
    rest = jnp.zeros((mode_dev, LANES - batches * nz), jnp.float32)
    both = jnp.concatenate(keys + [rest] + vals + [rest], axis=1)
    lanes2 = 2 * LANES
    both = choose(
        [m[:, :lanes2] for m in holds], [both[j : j + 1] for j in range(mode_dev)],
        (mode_dev, lanes2),
    )
    for c in range(batches):
        msg[c] = both[c * per_batch : (c + 1) * per_batch]
        allp[me, c] = both[c * per_batch : (c + 1) * per_batch]

    loads[4].wait()
    lines = []
    for n in range(slab_rows):
        lines.append(
            choose(
                holds, [force_v[pl.ds(j * slab_rows + n, 1), :] for j in range(mode_dev)],
                (mode_dev, ny),
            )
        )
    blank = jnp.zeros((mode_dev, steps), jnp.float32)
    for p in range(owners):
        start, stop = p * cols - steps, (p + 1) * cols + steps
        parts = []
        for line in lines:
            if start < 0:
                parts.append(blank)
            parts.append(line[:, max(start, 0) : min(stop, ny)])
            if stop > ny:
                parts.append(blank)
        flat = jnp.concatenate(parts, axis=1)
        for c in range(batches):
            win[p, c] = flat[c * per_batch : (c + 1) * per_batch]

    beside = has_low.astype(jnp.int32) + has_high.astype(jnp.int32)
    pl.semaphore_wait(barrier, owners - 1 + beside)
    for d in far:
        value_copy(0, d).start()
    for d in far:
        pair_copy(d).start()
    for c in range(1, batches):
        for d in far:
            value_copy(c, d).start()
    for c in range(batches):
        land[c, me, :, mid_at] = win[me, c]

    loads[5].wait()
    m = mean_v[...]
    place = lax.broadcasted_iota(jnp.int32, (slab_rows, ny), 1)
    level = lax.broadcasted_iota(jnp.int32, (slab_rows, ny), 0)
    right = jnp.where(place < ny - 1, pltpu.roll(m, ny - 1, 1), 0.0)
    left = jnp.where(place > 0, pltpu.roll(m, 1, 1), 0.0)
    after = jnp.where(level < slab_rows - 1, pltpu.roll(m, slab_rows - 1, 0), 0.0)
    before = jnp.where(level > 0, pltpu.roll(m, 1, 0), 0.0)
    for n, x in enumerate((m, 4.0 * m + right + left, before, after)):
        for h in range(halves):
            ext[h, pl.ds((fields + n) * slab_rows, slab_rows), :] = x[:, h * LANES : (h + 1) * LANES]
    for h in range(halves):
        loads[6 + h].wait()
    kpad = cbuf.shape[0]
    shift = lax.rem(ny - (me * cols - steps), ny)
    column = lax.broadcasted_iota(jnp.int32, (kpad, width), 1) + (me * cols - steps)
    real = (column >= 0) & (column < ny)
    parts = []
    for n in range(slab_rows):
        x = jnp.concatenate(
            [ext[h, pl.ds(n, kpad, stride=slab_rows), :] for h in range(halves)], axis=1
        )
        x = pltpu.roll(x, shift, 1)
        parts.append(jnp.where(real, x[:, :width], 0.0))
    cbuf[:, mid_at] = jnp.concatenate(parts, axis=1)
    pl.when(has_high)(lambda: coef_up().start())
    pl.when(has_low)(lambda: coef_down().start())

    def forward(c):
        for d in far:
            value_copy(c, d).wait_recv()
        pl.when(has_high)(lambda: up_copy(c).start())
        pl.when(has_low)(lambda: down_copy(c).start())

    pl.when(has_low)(lambda: coef_up().wait_recv())
    pl.when(has_high)(lambda: coef_down().wait_recv())
    a = cbuf[...]
    for n, hop in ((0, width), (2, 1)):
        face = 0.5 * (a + pltpu.roll(a, cells - hop, 1))
        faces[n] = face
        faces[n + 1] = pltpu.roll(face, hop, 1)
    centre, across = a[fields : fields + 1], a[fields + 1 : fields + 2]
    place = lax.broadcasted_iota(jnp.int32, (1, cells), 1)
    above = jnp.where(place < width, a[fields + 2 : fields + 3], pltpu.roll(centre, width, 1))
    below = jnp.where(
        place >= width * (rows - 1), a[fields + 3 : fields + 4],
        pltpu.roll(centre, cells - width, 1),
    )
    inside = across > 0.0
    diag = jnp.where(inside, 0.5 * (across + above + below), 1.0)
    inv[...] = jnp.where(inside, 1.0 / diag, 0.0)
    forward(0)
    for d in far:
        pair_copy(d).wait_recv()
    every = jnp.concatenate([allp[:, n].reshape(sources, 2 * LANES) for n in range(batches)], axis=0)
    span = batches // 2 * nz
    for n in range(2):
        one = every[:, n * LANES : (n + 1) * LANES]
        turn[n] = jnp.concatenate([one, pltpu.roll(one, LANES - span, 1)], axis=0).T
    code = turn[0]
    turn[2] = jnp.floor(code * (1.0 / sources))
    turn[0] = code - sources * turn[2]
    tile = (8, LANES)
    level = lax.broadcasted_iota(jnp.int32, tile, 0).astype(jnp.float32)
    part = fields // 2
    def fill(q):
        found = []
        for start in range(0, fields, part):
            sums = [[jnp.zeros(tile, jnp.float32)] * (sources // 8) for _ in range(part)]
            for z in range(nz):
                at = pl.ds(q * nz + z, 1)
                source, val, field = [jnp.broadcast_to(turn[n, at, :], tile) for n in range(3)]
                picks = [
                    jnp.where(source == level + float(8 * h), val, 0.0)
                    for h in range(sources // 8)
                ]
                for f in range(part):
                    hit = jnp.where(field == float(start + f), 1.0, 0.0)
                    sums[f] = [x + hit * y for x, y in zip(sums[f], picks)]
            found += [x for pair in sums for x in pair]
        found += [jnp.zeros(tile, jnp.float32)] * (w2.shape[2] // 8 - len(found))
        full = jnp.concatenate(found, axis=0).T
        hi = full.astype(jnp.bfloat16)
        mid = (full - hi.astype(jnp.float32)).astype(jnp.bfloat16)
        for h in range(2):
            c = q + h * (batches // 2)
            w2[c, pl.ds(0, modes), :] = hi[h * modes : (h + 1) * modes]
            w2[c, pl.ds(modes, modes), :] = mid[h * modes : (h + 1) * modes]

    fill(0)
    forward(1)
    forward(2)

    def compact(x):
        return jnp.concatenate(
            [x[:, q * width + steps : q * width + steps + cols] for q in range(slab_rows)], axis=1
        )

    pieces = tail.shape[0]
    piece = slab_rows // pieces
    sent = 0

    def ship(n):
        start = edge + n * piece * width
        for b in range(batches):
            x = r[pl.ds(b * sources, sources), :]
            done = jnp.concatenate(
                [
                    x[:, start + q * width + steps : start + q * width + steps + cols]
                    for q in range(piece)
                ],
                axis=1,
            )
            for o in range(owners):
                rpack[n, o, b] = done[o * per_batch : (o + 1) * per_batch]
        for d in far:
            residual_copy(n, d).start()
        tail[n, me] = rpack[n, me]

    groups = cells // LANES

    def arrived(c):
        pl.when(has_low)(lambda: up_copy(c).wait_recv())
        pl.when(has_high)(lambda: down_copy(c).wait_recv())

    def scaled(k, g):
        at = pl.ds(g * LANES, LANES)
        mine = pl.ds(k % batches * sources, sources)
        x = r[mine, at]
        if k < batches:
            x = x + land[k, :, :, at].reshape(sources, LANES)
            r[mine, at] = x
        ready[:, pl.ds((g + 1) * LANES, LANES)] = x * inv[:, at]

    def differ(k, g):
        wide = ready[:, pl.ds(g * LANES, 3 * LANES)]
        here = wide[:, LANES : 2 * LANES]
        for n, hop in ((0, width), (2, 1)):
            ahead = pltpu.roll(wide, 3 * LANES - hop, 1)[:, LANES : 2 * LANES]
            behind = pltpu.roll(wide, hop, 1)[:, LANES : 2 * LANES]
            diffs[k % 2, n, :, pl.ds(g * LANES, LANES)] = here - ahead
            diffs[k % 2, n + 1, :, pl.ds(g * LANES, LANES)] = behind - here

    def prepare(k):
        for g in range(groups):
            scaled(k, g)
            if g:
                differ(k, g - 1)
        differ(k, groups - 1)

    ready[...] = jnp.zeros_like(ready)
    arrived(0)
    prepare(0)
    for k in range(steps):
        c = k % batches
        first = (width * (k + 1)) // LANES
        last = -(-(width * (rows - 1 - k)) // LANES)
        mine = pl.ds(c * sources, sources)
        if k == 1:
            forward(3)
            fill(1)
            arrived(1)
            prepare(1)
        if 0 < k < batches - 1:
            arrived(k + 1)
        inner = ready[:, pl.ds(LANES + edge, core_cells)]
        if k < batches:
            sol[mine, :] = inner
        else:
            done = compact(sol[mine, :] + inner)
            for o in range(owners):
                spack[c, o] = done[o * per_batch : (o + 1) * per_batch]
            for d in far:
                solution_copy(c, d).start()
            back[c, me] = spack[c, me]

        depth = pl.ds(0, fields * sources)
        for g in range(first, last, WIDE):
            w = LANES * min(WIDE, last - g)
            at = pl.ds(g * LANES, w)
            near = [diffs[k % 2, n, :, at] for n in range(4)]
            his, mids = [], []
            for f in range(fields):
                a = [jnp.broadcast_to(faces[n, pl.ds(f, 1), at], (sources, w)) for n in range(4)]
                p = (a[0] * near[0] - a[1] * near[1]) + (a[2] * near[2] - a[3] * near[3])
                hi = p.astype(jnp.bfloat16)
                his.append(hi)
                mids.append((p - hi.astype(jnp.float32)).astype(jnp.bfloat16))
            got = jnp.dot(
                w2[c, :, depth], jnp.concatenate(his, axis=0), preferred_element_type=jnp.float32
            )
            more = jnp.dot(
                w2[c, pl.ds(0, modes), depth], jnp.concatenate(mids, axis=0),
                preferred_element_type=jnp.float32,
            )
            r[:, at] = r[:, at] - (got[:modes] + got[modes:] + more)
            if 0 < k < steps - 1:
                for h in range(g, g + w // LANES):
                    scaled(k + 1, h)
                    if h > first:
                        differ(k + 1, h - 1)
                if g + WIDE >= last:
                    differ(k + 1, last - 1)
            if k == steps - 1:
                while sent < pieces and edge + (sent + 1) * piece * width <= (g + WIDE) * LANES:
                    ship(sent)
                    sent += 1

    row_slot = jnp.zeros((mode_dev, ny), jnp.int32)
    for j in range(mode_dev):
        row_slot = jnp.where(sub == j, slots[j], row_slot)
    gives = [row_slot == s for s in range(mode_dev)]

    def restore(out, got, start, count):
        for n in range(count):
            line = jnp.concatenate([x[:, n * cols : (n + 1) * cols] for x in got], axis=1)
            line = choose(gives, [line[s : s + 1] for s in range(mode_dev)], (mode_dev, ny))
            at = start + n
            for h in range(halves):
                row = (at // 8 * halves + h) * 8 + at % 8
                out[pl.ds(row, mode_dev, stride=slab_rows * halves), :] = line[
                    :, h * LANES : (h + 1) * LANES
                ]

    for d in far:
        pair_copy(d).wait_send()
        for c in range(batches):
            value_copy(c, d).wait_send()
    for c in range(batches):
        pl.when(has_high)(lambda: up_copy(c).wait_send())
        pl.when(has_low)(lambda: down_copy(c).wait_send())
    pl.when(has_high)(lambda: coef_up().wait_send())
    pl.when(has_low)(lambda: coef_down().wait_send())
    for d in far:
        for c in range(batches):
            solution_copy(c, d).wait_send()
            solution_copy(c, d).wait_recv()
    got = [
        jnp.concatenate([back[c, p, :, : slab_rows * cols] for c in range(batches)], axis=0)
        for p in range(owners)
    ]
    restore(outs, got, 0, slab_rows)
    for n in range(pieces):
        for d in far:
            residual_copy(n, d).wait_send()
            residual_copy(n, d).wait_recv()
        got = [tail[n, p].reshape(mode_dev, piece * cols) for p in range(owners)]
        restore(sides, got, n * piece, piece)


def leave_kernel(outs, sides, first, second, sems):
    copies = [
        pltpu.make_async_copy(src, dst, sems.at[n])
        for n, (src, dst) in enumerate(((outs, first), (sides, second)))
    ]
    for one in copies:
        one.start()
    for one in copies:
        one.wait()


def patch_sizes(mesh, forcing, pair_src, coef_fields):
    owners = mesh.shape["mode"]
    slabs = mesh.shape["space"]
    modes, nx, ny = forcing.shape
    batches = pair_src.shape[0]
    nz = pair_src.shape[2]
    fields = coef_fields.shape[0]
    depth = SWEEPS * batches
    slab = nx // slabs
    cols = ny // owners
    width = cols + 2 * depth
    rows = slab + 2 * depth
    cells = rows * width
    sources = modes // batches
    fits = (
        slab > depth
        and cells % (2 * LANES) == 0
        and (slab * cols) % LANES == 0
        and (width * depth) % LANES == 0
        and width <= LANES
        and modes == 8 * owners
        and owners == 8
        and batches == 4
        and sources == 16
        and slab % 8 == 0
        and ny == 2 * LANES
        and fields <= 28
        and batches * nz <= LANES
    )
    return fits, (batches, sources, modes, width, depth, cells, rows, fields, nz, owners, slabs)


def by_patch(dims, forcing, mean_field, coef_fields, color, pair_src, pair_field, pair_value):
    batches, sources, modes, width, depth, cells, rows, fields, nz, owners, slabs = dims
    mode_dev, slab, ny = forcing.shape
    per_batch = mode_dev // batches
    cols = ny // owners
    core_cells = slab * width
    kpad = 32
    spread = -(-(fields * sources) // LANES) * LANES

    hbm = pl.BlockSpec(memory_space=pltpu.HBM)
    f32, i32 = jnp.float32, jnp.int32
    flat = pltpu.VMEM((mode_dev * slab * ny // LANES, LANES), f32)
    vmem = pl.BlockSpec(memory_space=pltpu.VMEM)
    sems = pltpu.SemaphoreType.DMA
    got = pl.pallas_call(
        functools.partial(sweep_kernel, dims),
        out_shape=(flat, flat),
        in_specs=[hbm] * 7,
        out_specs=(vmem, vmem),
        scratch_shapes=[
            pltpu.VMEM((3, LANES, LANES), f32),
            pltpu.SMEM((modes,), i32),
            pltpu.VMEM((batches, mode_dev, nz), i32),
            pltpu.VMEM((batches, mode_dev, nz), i32),
            pltpu.VMEM((batches, mode_dev, nz), f32),
            pltpu.VMEM((mode_dev * slab, ny), f32),
            pltpu.VMEM((slab, ny), f32),
            pltpu.VMEM((ny // LANES, kpad * slab, LANES), f32),
            pltpu.VMEM((batches, per_batch, 2 * LANES), f32),
            pltpu.VMEM((owners, batches, per_batch, 2 * LANES), f32),
            pltpu.VMEM((owners, batches, per_batch, core_cells), f32),
            pltpu.VMEM((batches, owners, per_batch, cells), f32),
            pltpu.VMEM((kpad, cells), f32),
            pltpu.VMEM((4, kpad, cells), f32),
            pltpu.VMEM((1, cells), f32),
            pltpu.VMEM((batches, 2 * modes, spread), jnp.bfloat16),
            pltpu.VMEM((modes, cells), f32),
            pltpu.VMEM((modes, core_cells), f32),
            pltpu.VMEM((sources, cells + 2 * LANES), f32),
            pltpu.VMEM((2, 4, sources, cells), f32),
            pltpu.VMEM((batches, owners, per_batch, slab * cols), f32),
            pltpu.VMEM((PIECES, owners, batches, per_batch, slab * cols // PIECES), f32),
            pltpu.VMEM((batches, owners, per_batch, slab * cols), f32),
            pltpu.VMEM((PIECES, owners, batches, per_batch, slab * cols // PIECES), f32),
            sems((8,)),
            sems((1 + 2 * batches + PIECES, owners)),
            sems((1 + 2 * batches + PIECES, owners)),
            sems((2, batches)),
            sems((2, batches)),
            sems((2,)),
            sems((2,)),
        ],
        compiler_params=pltpu.CompilerParams(
            collective_id=0, has_side_effects=True
        ),
        name="sweeps",
    )(
        color, pair_src, pair_field, pair_value, forcing.reshape(mode_dev * slab, ny), mean_field,
        coef_fields.reshape(fields * slab, ny),
    )
    plain = jax.ShapeDtypeStruct((mode_dev * slab * ny // LANES, LANES), f32)
    got = pl.pallas_call(
        leave_kernel,
        out_shape=(plain, plain),
        in_specs=[pl.BlockSpec(memory_space=pltpu.VMEM)] * 2,
        out_specs=(pl.BlockSpec(memory_space=pl.ANY),) * 2,
        scratch_shapes=[sems((2,))],
        compiler_params=pltpu.CompilerParams(vmem_limit_bytes=4_000_000),
        name="leave",
    )(*got)
    shape = (mode_dev * slab // 8, ny // LANES, 8, LANES)
    return tuple(
        x.reshape(shape).transpose(0, 2, 1, 3).reshape(mode_dev, slab, ny) for x in got
    )


def solution(mesh):
    specs = (
        P("mode", "space", None),
        P("space", None),
        P(None, "space", None),
        P(),
        P(None, "mode", None),
        P(None, "mode", None),
        P(None, "mode", None),
    )

    def whole(*args):
        fits, dims = patch_sizes(mesh, args[0], args[4], args[2])
        body = functools.partial(by_patch, dims) if fits else by_batch
        return jax.shard_map(
            body,
            mesh=mesh,
            in_specs=specs,
            out_specs=(P("mode", "space", None), P("mode", "space", None)),
            check_vma=False,
        )(*args)

    return whole
```

```python
import functools

import jax
import jax.numpy as jnp
from jax import lax
from jax.experimental import pallas as pl
from jax.experimental.pallas import tpu as pltpu
from jax.sharding import PartitionSpec as P

SWEEPS = 2
LANES = 128
PIECES = 2
WIDE = 2


def with_halo(block, sides, width):
    for axis, dim in sides:
        count = lax.axis_size(axis)
        forward = [(i, i + 1) for i in range(count - 1)]
        backward = [(target, source) for source, target in forward]
        low = lax.ppermute(
            lax.slice_in_dim(block, block.shape[dim] - width, None, axis=dim), axis, forward
        )
        high = lax.ppermute(lax.slice_in_dim(block, 0, width, axis=dim), axis, backward)
        block = jnp.concatenate([low, block, high], axis=dim)
    return block


def stencil_ext(coeff_ext, value_ext):
    coeff_mid = coeff_ext[1:-1]
    value_mid = value_ext[1:-1]
    coeff_side = jnp.pad(coeff_mid, ((0, 0), (1, 1)))
    value_side = jnp.pad(value_mid, ((0, 0), (1, 1)))
    result = 0.5 * (coeff_mid + coeff_ext[2:]) * (value_mid - value_ext[2:])
    result = result + 0.5 * (coeff_mid + coeff_ext[:-2]) * (value_mid - value_ext[:-2])
    result = result + 0.5 * (coeff_mid + coeff_side[:, 2:]) * (value_mid - value_side[:, 2:])
    result = result + 0.5 * (coeff_mid + coeff_side[:, :-2]) * (value_mid - value_side[:, :-2])
    return result


def face_sum_ext(coeff_ext):
    coeff_mid = coeff_ext[1:-1]
    coeff_side = jnp.pad(coeff_mid, ((0, 0), (1, 1)))
    result = 0.5 * (coeff_mid + coeff_ext[2:])
    result = result + 0.5 * (coeff_mid + coeff_ext[:-2])
    result = result + 0.5 * (coeff_mid + coeff_side[:, 2:])
    result = result + 0.5 * (coeff_mid + coeff_side[:, :-2])
    return result


def couple(gathered, sources, field_ids, weights, stacked_ext):

    def reader(reader_entry):
        source_rows, field_rows, weight_rows = reader_entry
        values = jnp.take(gathered, source_rows, axis=0)
        coeffs = jnp.take(stacked_ext, field_rows + 1, axis=0)
        fluxes = jax.vmap(stencil_ext)(coeffs, values)
        return jnp.sum(weight_rows[:, None, None] * fluxes, axis=0)

    return lax.map(reader, (sources, field_ids, weights))


def ranks(color, mode_dev, batches):
    grouped = color.reshape(-1, mode_dev)
    onehot = (grouped[:, :, None] == jnp.arange(batches, dtype=jnp.int32)[None, None, :]).astype(
        jnp.int32
    )
    earlier = jnp.cumsum(onehot, axis=1) - onehot
    return jnp.sum(onehot * earlier, axis=2).reshape(-1)


def by_batch(forcing, mean_field, coef_fields, color, pair_src, pair_field, pair_value):
    mode_dev = forcing.shape[0]
    batches = pair_src.shape[0]
    per_batch = mode_dev // batches
    stacked = jnp.concatenate([mean_field[None], coef_fields], axis=0)
    stacked_ext = with_halo(stacked, (("space", 1),), 1)
    diag_sum = face_sum_ext(stacked_ext[0])
    ranking = ranks(color, mode_dev, batches)
    owners = jnp.arange(color.shape[0], dtype=jnp.int32) // mode_dev
    pool_rows = owners * per_batch + ranking
    source_rows = jnp.take(pool_rows, pair_src, axis=0)
    offset = lax.axis_index("mode") * mode_dev
    local_color = lax.dynamic_slice_in_dim(color, offset, mode_dev)
    local_rank = lax.dynamic_slice_in_dim(ranking, offset, mode_dev)
    positions = jnp.arange(mode_dev, dtype=jnp.int32)
    slot_numbers = jnp.arange(per_batch, dtype=jnp.int32)
    solution = jnp.zeros(forcing.shape, jnp.float32)
    coupled = jnp.zeros(forcing.shape, jnp.float32)
    for sweep_idx in range(SWEEPS):
        for color_idx in range(batches):
            active = local_color == color_idx
            update = jnp.where(active[:, None, None], (forcing - coupled) / diag_sum, 0.0)
            solution = solution + update
            selected = (active[None, :] & (local_rank[None, :] == slot_numbers[:, None])).astype(
                jnp.int32
            )
            chosen = jnp.sum(positions[None, :] * selected, axis=1)
            own_update = jnp.take(update, chosen, axis=0)
            inner = lax.all_gather(own_update, "mode", axis=0, tiled=True)
            gathered = with_halo(inner, (("space", 1),), 1)
            coupled = coupled + couple(
                gathered,
                source_rows[color_idx],
                pair_field[color_idx],
                pair_value[color_idx],
                stacked_ext,
            )
    return (solution, forcing - coupled)


def sweep_kernel(dims, color, psrc, pfield, pval, forcing, mean, coef, outs, sides,
                 turn, shade, src_v, field_v, val_v, force_v, mean_v, ext, msg, allp, win, land, cbuf, faces,
                 inv, w2, r, sol, ready, diffs, spack, rpack, back, tail, local, send, recv, hsend, hrecv,
                 csend, crecv):
    batches, sources, modes, width, steps, cells, rows, fields, nz, owners, slabs = dims
    mode_dev = modes // owners
    per_batch = mode_dev // batches
    edge = width * steps
    core_cells = cells - 2 * edge
    slab_rows = core_cells // width
    cols = width - 2 * steps
    ny = cols * owners
    me = lax.axis_index("mode")
    slab = lax.axis_index("space")
    low, mid_at, high = pl.ds(0, edge), pl.ds(edge, core_cells), pl.ds(cells - edge, edge)
    has_low, has_high = slab > 0, slab < slabs - 1

    def peer(d):
        at = me
        bit = 1
        while bit < owners:
            if d & bit:
                at = at + bit * (1 - 2 * (me // bit % 2))
            bit *= 2
        return at

    far = range(owners - 1, 0, -1)

    barrier = pltpu.get_barrier_semaphore()
    for d in far:
        pl.semaphore_signal(
            barrier, inc=1, device_id={"mode": peer(d)}, device_id_type=pl.DeviceIdType.MESH
        )
    for there, at in ((has_low, slab - 1), (has_high, slab + 1)):

        @pl.when(there)
        def _():
            pl.semaphore_signal(
                barrier, inc=1, device_id={"space": at}, device_id_type=pl.DeviceIdType.MESH
            )

    def remote(src, dst, ssem, rsem, **where):
        return pltpu.make_async_remote_copy(
            src_ref=src, dst_ref=dst, send_sem=ssem, recv_sem=rsem, device_id=where,
            device_id_type=pl.DeviceIdType.MESH,
        )

    def pair_copy(q, d):
        sem = 0 if q == 0 else 1 + 2 * batches + tail.shape[0]
        return remote(
            msg.at[q], allp.at[q, me], send.at[sem, d], recv.at[sem, d], mode=peer(d)
        )

    def value_copy(c, d):
        return remote(
            win.at[peer(d), c], land.at[c, me, :, mid_at], send.at[1 + c, d], recv.at[1 + c, d],
            mode=peer(d),
        )

    def up_copy(c):
        return remote(
            land.at[c, :, :, pl.ds(core_cells, edge)], land.at[c, :, :, low],
            hsend.at[0, c], hrecv.at[0, c], space=slab + 1,
        )

    def down_copy(c):
        return remote(
            land.at[c, :, :, pl.ds(edge, edge)], land.at[c, :, :, high],
            hsend.at[1, c], hrecv.at[1, c], space=slab - 1,
        )

    def coef_up():
        return remote(
            cbuf.at[:, pl.ds(core_cells, edge)], cbuf.at[:, low], csend.at[0], crecv.at[0],
            space=slab + 1,
        )

    def coef_down():
        return remote(
            cbuf.at[:, pl.ds(edge, edge)], cbuf.at[:, high], csend.at[1], crecv.at[1],
            space=slab - 1,
        )

    def solution_copy(c, d):
        return remote(
            spack.at[c, peer(d)], back.at[c, me], send.at[1 + batches + c, d],
            recv.at[1 + batches + c, d], mode=peer(d),
        )

    def residual_copy(n, d):
        return remote(
            rpack.at[n, peer(d)], tail.at[n, me], send.at[1 + 2 * batches + n, d],
            recv.at[1 + 2 * batches + n, d], mode=peer(d),
        )

    loads = [
        pltpu.make_async_copy(src, dst, local.at[n])
        for n, (src, dst) in enumerate(
            (
                (color, shade), (psrc, src_v), (pfield, field_v), (pval, val_v),
                (forcing, force_v), (mean, mean_v),
            )
        )
    ]
    halves = ny // LANES
    for h in range(halves):
        part = pl.ds(h * LANES, LANES)
        loads.append(
            pltpu.make_async_copy(
                coef.at[:, part], ext.at[h, pl.ds(0, fields * slab_rows)], local.at[6 + h]
            )
        )
    for one in loads:
        one.start()

    for there, at in ((has_low, low), (has_high, high)):

        @pl.when(jnp.logical_not(there))
        def _():
            for c in range(batches):
                land[c, :, :, at] = jnp.zeros((owners, per_batch, edge), jnp.float32)
            cbuf[:, at] = jnp.zeros((cbuf.shape[0], edge), jnp.float32)

    r[...] = jnp.zeros_like(r)

    def earlier(shades, j):
        found = jnp.int32(0)
        for i in range(j):
            found = found | (shades[i] == shades[j]).astype(jnp.int32)
        return found

    loads[0].wait()
    second = []
    for o in range(owners):
        shades = [shade[o * mode_dev + j] for j in range(mode_dev)]
        second.append(
            functools.reduce(
                lambda x, y: x | y, [earlier(shades, j) << j for j in range(1, mode_dev)]
            )
        )
    shades = [shade[me * mode_dev + j] for j in range(mode_dev)]
    slots = [shades[j] * per_batch + earlier(shades, j) for j in range(mode_dev)]
    sub = lax.broadcasted_iota(jnp.int32, (mode_dev, ny), 0)
    holds = [sub == slots[j] for j in range(mode_dev)]

    def choose(masks, lines, shape):
        out = jnp.broadcast_to(lines[0], shape)
        for j in range(1, mode_dev):
            out = jnp.where(masks[j], jnp.broadcast_to(lines[j], shape), out)
        return out

    for n in (1, 2, 3):
        loads[n].wait()
    keys, vals = [], []
    for c in range(batches):
        src = src_v[c]
        owner = src >> 3
        bits = jnp.zeros_like(src)
        for o in range(owners):
            bits = jnp.where(owner == o, second[o], bits)
        source = owner * per_batch + ((bits >> (src & 7)) & 1)
        keys.append((field_v[c] * sources + source).astype(jnp.float32))
        vals.append(val_v[c])
    apart = batches // 2
    rest = jnp.zeros((mode_dev, LANES - batches * nz), jnp.float32)
    both = jnp.concatenate(
        [
            x
            for q in range(apart)
            for x in [keys[q], keys[q + apart], vals[q], vals[q + apart], rest]
        ],
        axis=1,
    )
    both = choose(
        [m[:, : apart * LANES] for m in holds], [both[j : j + 1] for j in range(mode_dev)],
        (mode_dev, apart * LANES),
    )
    for q in range(apart):
        for c in range(batches):
            one = both[c * per_batch : (c + 1) * per_batch, q * LANES : (q + 1) * LANES]
            msg[q, c] = one
            allp[q, me, c] = one

    loads[4].wait()
    lines = []
    for n in range(slab_rows):
        lines.append(
            choose(
                holds, [force_v[pl.ds(j * slab_rows + n, 1), :] for j in range(mode_dev)],
                (mode_dev, ny),
            )
        )
    blank = jnp.zeros((mode_dev, steps), jnp.float32)
    for p in range(owners):
        start, stop = p * cols - steps, (p + 1) * cols + steps
        parts = []
        for line in lines:
            if start < 0:
                parts.append(blank)
            parts.append(line[:, max(start, 0) : min(stop, ny)])
            if stop > ny:
                parts.append(blank)
        flat = jnp.concatenate(parts, axis=1)
        for c in range(batches):
            win[p, c] = flat[c * per_batch : (c + 1) * per_batch]

    beside = has_low.astype(jnp.int32) + has_high.astype(jnp.int32)
    pl.semaphore_wait(barrier, owners - 1 + beside)
    for d in far:
        value_copy(0, d).start()
    for d in far:
        pair_copy(0, d).start()
    for d in far:
        value_copy(1, d).start()
    for d in far:
        pair_copy(1, d).start()
    for c in range(2, batches):
        for d in far:
            value_copy(c, d).start()
    for c in range(batches):
        land[c, me, :, mid_at] = win[me, c]

    loads[5].wait()
    m = mean_v[...]
    place = lax.broadcasted_iota(jnp.int32, (slab_rows, ny), 1)
    level = lax.broadcasted_iota(jnp.int32, (slab_rows, ny), 0)
    right = jnp.where(place < ny - 1, pltpu.roll(m, ny - 1, 1), 0.0)
    left = jnp.where(place > 0, pltpu.roll(m, 1, 1), 0.0)
    after = jnp.where(level < slab_rows - 1, pltpu.roll(m, slab_rows - 1, 0), 0.0)
    before = jnp.where(level > 0, pltpu.roll(m, 1, 0), 0.0)
    for n, x in enumerate((m, 4.0 * m + right + left, before, after)):
        for h in range(halves):
            ext[h, pl.ds((fields + n) * slab_rows, slab_rows), :] = x[:, h * LANES : (h + 1) * LANES]
    for h in range(halves):
        loads[6 + h].wait()
    kpad = cbuf.shape[0]
    shift = lax.rem(ny - (me * cols - steps), ny)
    column = lax.broadcasted_iota(jnp.int32, (kpad, width), 1) + (me * cols - steps)
    real = (column >= 0) & (column < ny)
    parts = []
    for n in range(slab_rows):
        x = jnp.concatenate(
            [ext[h, pl.ds(n, kpad, stride=slab_rows), :] for h in range(halves)], axis=1
        )
        x = pltpu.roll(x, shift, 1)
        parts.append(jnp.where(real, x[:, :width], 0.0))
    cbuf[:, mid_at] = jnp.concatenate(parts, axis=1)
    pl.when(has_high)(lambda: coef_up().start())
    pl.when(has_low)(lambda: coef_down().start())

    def forward(c):
        for d in far:
            value_copy(c, d).wait_recv()
        pl.when(has_high)(lambda: up_copy(c).start())
        pl.when(has_low)(lambda: down_copy(c).start())

    pl.when(has_low)(lambda: coef_up().wait_recv())
    pl.when(has_high)(lambda: coef_down().wait_recv())
    a = cbuf[...]
    for n, hop in ((0, width), (2, 1)):
        face = 0.5 * (a + pltpu.roll(a, cells - hop, 1))
        faces[n] = face
        faces[n + 1] = pltpu.roll(face, hop, 1)
    centre, across = a[fields : fields + 1], a[fields + 1 : fields + 2]
    place = lax.broadcasted_iota(jnp.int32, (1, cells), 1)
    above = jnp.where(place < width, a[fields + 2 : fields + 3], pltpu.roll(centre, width, 1))
    below = jnp.where(
        place >= width * (rows - 1), a[fields + 3 : fields + 4],
        pltpu.roll(centre, cells - width, 1),
    )
    inside = across > 0.0
    diag = jnp.where(inside, 0.5 * (across + above + below), 1.0)
    inv[...] = jnp.where(inside, 1.0 / diag, 0.0)
    forward(0)
    tile = (8, LANES)
    level = lax.broadcasted_iota(jnp.int32, tile, 0).astype(jnp.float32)
    part = fields // 2
    def fill(q):
        for d in far:
            pair_copy(q, d).wait_recv()
        every = jnp.concatenate(
            [allp[q, :, n].reshape(sources, LANES) for n in range(batches)], axis=0
        )
        turn[0] = jnp.concatenate([every, pltpu.roll(every, LANES - nz, 1)], axis=0).T
        code = turn[0, pl.ds(0, nz), :]
        turn[1, pl.ds(0, nz), :] = jnp.floor(code * (1.0 / sources))
        turn[2, pl.ds(0, nz), :] = code - sources * turn[1, pl.ds(0, nz), :]
        found = []
        for start in range(0, fields, part):
            sums = [[jnp.zeros(tile, jnp.float32)] * (sources // 8) for _ in range(part)]
            for z in range(nz):
                val, field, source = [
                    jnp.broadcast_to(turn[n, pl.ds(at, 1), :], tile)
                    for n, at in ((0, 2 * nz + z), (1, z), (2, z))
                ]
                picks = [
                    jnp.where(source == level + float(8 * h), val, 0.0)
                    for h in range(sources // 8)
                ]
                for f in range(part):
                    hit = jnp.where(field == float(start + f), 1.0, 0.0)
                    sums[f] = [x + hit * y for x, y in zip(sums[f], picks)]
            found += sums
        found = [x[h] for h in range(sources // 8) for x in found]
        found += [jnp.zeros(tile, jnp.float32)] * (w2.shape[2] // 8 - len(found))
        full = jnp.concatenate(found, axis=0).T
        hi = full.astype(jnp.bfloat16)
        mid = (full - hi.astype(jnp.float32)).astype(jnp.bfloat16)
        for h in range(2):
            c = q + h * (batches // 2)
            w2[c, pl.ds(0, modes), :] = hi[h * modes : (h + 1) * modes]
            w2[c, pl.ds(modes, modes), :] = mid[h * modes : (h + 1) * modes]

    fill(0)
    forward(1)

    def compact(x):
        return jnp.concatenate(
            [x[:, q * width + steps : q * width + steps + cols] for q in range(slab_rows)], axis=1
        )

    pieces = tail.shape[0]
    piece = slab_rows // pieces
    sent = 0

    def ship(n):
        start = edge + n * piece * width
        for b in range(batches):
            x = r[pl.ds(b * sources, sources), :]
            done = jnp.concatenate(
                [
                    x[:, start + q * width + steps : start + q * width + steps + cols]
                    for q in range(piece)
                ],
                axis=1,
            )
            for o in range(owners):
                rpack[n, o, b] = done[o * per_batch : (o + 1) * per_batch]
        for d in far:
            residual_copy(n, d).start()
        tail[n, me] = rpack[n, me]

    groups = cells // LANES

    def arrived(c):
        pl.when(has_low)(lambda: up_copy(c).wait_recv())
        pl.when(has_high)(lambda: down_copy(c).wait_recv())

    def scaled(k, g):
        at = pl.ds(g * LANES, LANES)
        mine = pl.ds(k % batches * sources, sources)
        x = r[mine, at]
        if k < batches:
            x = x + land[k, :, :, at].reshape(sources, LANES)
            r[mine, at] = x
        ready[:, pl.ds((g + 1) * LANES, LANES)] = x * inv[:, at]

    def differ(k, g):
        wide = ready[:, pl.ds(g * LANES, 3 * LANES)]
        here = wide[:, LANES : 2 * LANES]
        for n, hop in ((0, width), (2, 1)):
            ahead = pltpu.roll(wide, 3 * LANES - hop, 1)[:, LANES : 2 * LANES]
            behind = pltpu.roll(wide, hop, 1)[:, LANES : 2 * LANES]
            diffs[k % 2, n, :, pl.ds(g * LANES, LANES)] = here - ahead
            diffs[k % 2, n + 1, :, pl.ds(g * LANES, LANES)] = behind - here

    def prepare(k):
        for g in range(groups):
            scaled(k, g)
            if g:
                differ(k, g - 1)
        differ(k, groups - 1)

    ready[...] = jnp.zeros_like(ready)
    arrived(0)
    prepare(0)
    for k in range(steps):
        c = k % batches
        first = (width * (k + 1)) // LANES
        last = -(-(width * (rows - 1 - k)) // LANES)
        mine = pl.ds(c * sources, sources)
        if k == 1:
            forward(2)
            fill(1)
            forward(3)
        if k in (1, 2):
            arrived(k)
            prepare(k)
        if k == 2:
            arrived(3)
        inner = ready[:, pl.ds(LANES + edge, core_cells)]
        if k < batches:
            sol[mine, :] = inner
        else:
            done = compact(sol[mine, :] + inner)
            for o in range(owners):
                spack[c, o] = done[o * per_batch : (o + 1) * per_batch]
            for d in far:
                solution_copy(c, d).start()
            back[c, me] = spack[c, me]

        depth = pl.ds(0, fields * sources)
        for g in range(first, last, WIDE):
            w = LANES * min(WIDE, last - g)
            at = pl.ds(g * LANES, w)
            his, mids = [], []
            for h in range(sources // 8):
                near = [diffs[k % 2, n, pl.ds(h * 8, 8), at] for n in range(4)]
                for f in range(0, fields, 2):
                    pair = []
                    for e in (f, f + 1):
                        a = [jnp.broadcast_to(faces[n, pl.ds(e, 1), at], (8, w)) for n in range(4)]
                        pair.append((a[0] * near[0] - a[1] * near[1]) + (a[2] * near[2] - a[3] * near[3]))
                    p = jnp.concatenate(pair, axis=0)
                    hi = p.astype(jnp.bfloat16)
                    his.append(hi)
                    mids.append((p - hi.astype(jnp.float32)).astype(jnp.bfloat16))
            got = jnp.dot(
                w2[c, :, depth], jnp.concatenate(his, axis=0), preferred_element_type=jnp.float32
            )
            more = jnp.dot(
                w2[c, pl.ds(0, modes), depth], jnp.concatenate(mids, axis=0),
                preferred_element_type=jnp.float32,
            )
            r[:, at] = r[:, at] - (got[:modes] + got[modes:] + more)
            if 1 < k < steps - 1:
                for h in range(g, g + w // LANES):
                    scaled(k + 1, h)
                    if h > first:
                        differ(k + 1, h - 1)
                if g + WIDE >= last:
                    differ(k + 1, last - 1)
            if k == steps - 1:
                while sent < pieces and edge + (sent + 1) * piece * width <= (g + WIDE) * LANES:
                    ship(sent)
                    sent += 1

    row_slot = jnp.zeros((mode_dev, ny), jnp.int32)
    for j in range(mode_dev):
        row_slot = jnp.where(sub == j, slots[j], row_slot)
    gives = [row_slot == s for s in range(mode_dev)]

    def restore(out, got, start, count):
        for n in range(count):
            line = jnp.concatenate([x[:, n * cols : (n + 1) * cols] for x in got], axis=1)
            line = choose(gives, [line[s : s + 1] for s in range(mode_dev)], (mode_dev, ny))
            at = start + n
            for h in range(halves):
                row = (at // 8 * halves + h) * 8 + at % 8
                out[pl.ds(row, mode_dev, stride=slab_rows * halves), :] = line[
                    :, h * LANES : (h + 1) * LANES
                ]

    for d in far:
        for q in range(apart):
            pair_copy(q, d).wait_send()
        for c in range(batches):
            value_copy(c, d).wait_send()
    for c in range(batches):
        pl.when(has_high)(lambda: up_copy(c).wait_send())
        pl.when(has_low)(lambda: down_copy(c).wait_send())
    pl.when(has_high)(lambda: coef_up().wait_send())
    pl.when(has_low)(lambda: coef_down().wait_send())
    for d in far:
        for c in range(batches):
            solution_copy(c, d).wait_send()
            solution_copy(c, d).wait_recv()
    got = [
        jnp.concatenate([back[c, p, :, : slab_rows * cols] for c in range(batches)], axis=0)
        for p in range(owners)
    ]
    restore(outs, got, 0, slab_rows)
    for n in range(pieces):
        for d in far:
            residual_copy(n, d).wait_send()
            residual_copy(n, d).wait_recv()
        got = [tail[n, p].reshape(mode_dev, piece * cols) for p in range(owners)]
        restore(sides, got, n * piece, piece)


def leave_kernel(outs, sides, first, second, sems):
    copies = [
        pltpu.make_async_copy(src, dst, sems.at[n])
        for n, (src, dst) in enumerate(((outs, first), (sides, second)))
    ]
    for one in copies:
        one.start()
    for one in copies:
        one.wait()


def patch_sizes(mesh, forcing, pair_src, coef_fields):
    owners = mesh.shape["mode"]
    slabs = mesh.shape["space"]
    modes, nx, ny = forcing.shape
    batches = pair_src.shape[0]
    nz = pair_src.shape[2]
    fields = coef_fields.shape[0]
    depth = SWEEPS * batches
    slab = nx // slabs
    cols = ny // owners
    width = cols + 2 * depth
    rows = slab + 2 * depth
    cells = rows * width
    sources = modes // batches
    fits = (
        slab > depth
        and cells % (2 * LANES) == 0
        and (slab * cols) % LANES == 0
        and (width * depth) % LANES == 0
        and width <= LANES
        and modes == 8 * owners
        and owners == 8
        and batches == 4
        and sources == 16
        and slab % 8 == 0
        and ny == 2 * LANES
        and fields <= 28
        and batches * nz <= LANES
    )
    return fits, (batches, sources, modes, width, depth, cells, rows, fields, nz, owners, slabs)


def by_patch(dims, forcing, mean_field, coef_fields, color, pair_src, pair_field, pair_value):
    batches, sources, modes, width, depth, cells, rows, fields, nz, owners, slabs = dims
    mode_dev, slab, ny = forcing.shape
    per_batch = mode_dev // batches
    cols = ny // owners
    core_cells = slab * width
    kpad = 32
    spread = -(-(fields * sources) // LANES) * LANES

    hbm = pl.BlockSpec(memory_space=pltpu.HBM)
    f32, i32 = jnp.float32, jnp.int32
    flat = pltpu.VMEM((mode_dev * slab * ny // LANES, LANES), f32)
    vmem = pl.BlockSpec(memory_space=pltpu.VMEM)
    sems = pltpu.SemaphoreType.DMA
    got = pl.pallas_call(
        functools.partial(sweep_kernel, dims),
        out_shape=(flat, flat),
        in_specs=[hbm] * 7,
        out_specs=(vmem, vmem),
        scratch_shapes=[
            pltpu.VMEM((3, LANES, LANES), f32),
            pltpu.SMEM((modes,), i32),
            pltpu.VMEM((batches, mode_dev, nz), i32),
            pltpu.VMEM((batches, mode_dev, nz), i32),
            pltpu.VMEM((batches, mode_dev, nz), f32),
            pltpu.VMEM((mode_dev * slab, ny), f32),
            pltpu.VMEM((slab, ny), f32),
            pltpu.VMEM((ny // LANES, kpad * slab, LANES), f32),
            pltpu.VMEM((batches // 2, batches, per_batch, LANES), f32),
            pltpu.VMEM((batches // 2, owners, batches, per_batch, LANES), f32),
            pltpu.VMEM((owners, batches, per_batch, core_cells), f32),
            pltpu.VMEM((batches, owners, per_batch, cells), f32),
            pltpu.VMEM((kpad, cells), f32),
            pltpu.VMEM((4, kpad, cells), f32),
            pltpu.VMEM((1, cells), f32),
            pltpu.VMEM((batches, 2 * modes, spread), jnp.bfloat16),
            pltpu.VMEM((modes, cells), f32),
            pltpu.VMEM((modes, core_cells), f32),
            pltpu.VMEM((sources, cells + 2 * LANES), f32),
            pltpu.VMEM((2, 4, sources, cells), f32),
            pltpu.VMEM((batches, owners, per_batch, slab * cols), f32),
            pltpu.VMEM((PIECES, owners, batches, per_batch, slab * cols // PIECES), f32),
            pltpu.VMEM((batches, owners, per_batch, slab * cols), f32),
            pltpu.VMEM((PIECES, owners, batches, per_batch, slab * cols // PIECES), f32),
            sems((8,)),
            sems((2 + 2 * batches + PIECES, owners)),
            sems((2 + 2 * batches + PIECES, owners)),
            sems((2, batches)),
            sems((2, batches)),
            sems((2,)),
            sems((2,)),
        ],
        compiler_params=pltpu.CompilerParams(
            collective_id=0, has_side_effects=True
        ),
        name="sweeps",
    )(
        color, pair_src, pair_field, pair_value, forcing.reshape(mode_dev * slab, ny), mean_field,
        coef_fields.reshape(fields * slab, ny),
    )
    plain = jax.ShapeDtypeStruct((mode_dev * slab * ny // LANES, LANES), f32)
    got = pl.pallas_call(
        leave_kernel,
        out_shape=(plain, plain),
        in_specs=[pl.BlockSpec(memory_space=pltpu.VMEM)] * 2,
        out_specs=(pl.BlockSpec(memory_space=pl.ANY),) * 2,
        scratch_shapes=[sems((2,))],
        compiler_params=pltpu.CompilerParams(vmem_limit_bytes=4_000_000),
        name="leave",
    )(*got)
    shape = (mode_dev * slab // 8, ny // LANES, 8, LANES)
    return tuple(
        x.reshape(shape).transpose(0, 2, 1, 3).reshape(mode_dev, slab, ny) for x in got
    )


def solution(mesh):
    specs = (
        P("mode", "space", None),
        P("space", None),
        P(None, "space", None),
        P(),
        P(None, "mode", None),
        P(None, "mode", None),
        P(None, "mode", None),
    )

    def whole(*args):
        fits, dims = patch_sizes(mesh, args[0], args[4], args[2])
        body = functools.partial(by_patch, dims) if fits else by_batch
        return jax.shard_map(
            body,
            mesh=mesh,
            in_specs=specs,
            out_specs=(P("mode", "space", None), P("mode", "space", None)),
            check_vma=False,
        )(*args)

    return whole
```

```python
import functools

import jax
import jax.numpy as jnp
from jax import lax
from jax.experimental import pallas as pl
from jax.experimental.pallas import tpu as pltpu
from jax.sharding import PartitionSpec as P

SWEEPS = 2
LANES = 128
PIECES = 2
WIDE = 2


def with_halo(block, sides, width):
    for axis, dim in sides:
        count = lax.axis_size(axis)
        forward = [(i, i + 1) for i in range(count - 1)]
        backward = [(target, source) for source, target in forward]
        low = lax.ppermute(
            lax.slice_in_dim(block, block.shape[dim] - width, None, axis=dim), axis, forward
        )
        high = lax.ppermute(lax.slice_in_dim(block, 0, width, axis=dim), axis, backward)
        block = jnp.concatenate([low, block, high], axis=dim)
    return block


def stencil_ext(coeff_ext, value_ext):
    coeff_mid = coeff_ext[1:-1]
    value_mid = value_ext[1:-1]
    coeff_side = jnp.pad(coeff_mid, ((0, 0), (1, 1)))
    value_side = jnp.pad(value_mid, ((0, 0), (1, 1)))
    result = 0.5 * (coeff_mid + coeff_ext[2:]) * (value_mid - value_ext[2:])
    result = result + 0.5 * (coeff_mid + coeff_ext[:-2]) * (value_mid - value_ext[:-2])
    result = result + 0.5 * (coeff_mid + coeff_side[:, 2:]) * (value_mid - value_side[:, 2:])
    result = result + 0.5 * (coeff_mid + coeff_side[:, :-2]) * (value_mid - value_side[:, :-2])
    return result


def face_sum_ext(coeff_ext):
    coeff_mid = coeff_ext[1:-1]
    coeff_side = jnp.pad(coeff_mid, ((0, 0), (1, 1)))
    result = 0.5 * (coeff_mid + coeff_ext[2:])
    result = result + 0.5 * (coeff_mid + coeff_ext[:-2])
    result = result + 0.5 * (coeff_mid + coeff_side[:, 2:])
    result = result + 0.5 * (coeff_mid + coeff_side[:, :-2])
    return result


def couple(gathered, sources, field_ids, weights, stacked_ext):

    def reader(reader_entry):
        source_rows, field_rows, weight_rows = reader_entry
        values = jnp.take(gathered, source_rows, axis=0)
        coeffs = jnp.take(stacked_ext, field_rows + 1, axis=0)
        fluxes = jax.vmap(stencil_ext)(coeffs, values)
        return jnp.sum(weight_rows[:, None, None] * fluxes, axis=0)

    return lax.map(reader, (sources, field_ids, weights))


def ranks(color, mode_dev, batches):
    grouped = color.reshape(-1, mode_dev)
    onehot = (grouped[:, :, None] == jnp.arange(batches, dtype=jnp.int32)[None, None, :]).astype(
        jnp.int32
    )
    earlier = jnp.cumsum(onehot, axis=1) - onehot
    return jnp.sum(onehot * earlier, axis=2).reshape(-1)


def by_batch(forcing, mean_field, coef_fields, color, pair_src, pair_field, pair_value):
    mode_dev = forcing.shape[0]
    batches = pair_src.shape[0]
    per_batch = mode_dev // batches
    stacked = jnp.concatenate([mean_field[None], coef_fields], axis=0)
    stacked_ext = with_halo(stacked, (("space", 1),), 1)
    diag_sum = face_sum_ext(stacked_ext[0])
    ranking = ranks(color, mode_dev, batches)
    owners = jnp.arange(color.shape[0], dtype=jnp.int32) // mode_dev
    pool_rows = owners * per_batch + ranking
    source_rows = jnp.take(pool_rows, pair_src, axis=0)
    offset = lax.axis_index("mode") * mode_dev
    local_color = lax.dynamic_slice_in_dim(color, offset, mode_dev)
    local_rank = lax.dynamic_slice_in_dim(ranking, offset, mode_dev)
    positions = jnp.arange(mode_dev, dtype=jnp.int32)
    slot_numbers = jnp.arange(per_batch, dtype=jnp.int32)
    solution = jnp.zeros(forcing.shape, jnp.float32)
    coupled = jnp.zeros(forcing.shape, jnp.float32)
    for sweep_idx in range(SWEEPS):
        for color_idx in range(batches):
            active = local_color == color_idx
            update = jnp.where(active[:, None, None], (forcing - coupled) / diag_sum, 0.0)
            solution = solution + update
            selected = (active[None, :] & (local_rank[None, :] == slot_numbers[:, None])).astype(
                jnp.int32
            )
            chosen = jnp.sum(positions[None, :] * selected, axis=1)
            own_update = jnp.take(update, chosen, axis=0)
            inner = lax.all_gather(own_update, "mode", axis=0, tiled=True)
            gathered = with_halo(inner, (("space", 1),), 1)
            coupled = coupled + couple(
                gathered,
                source_rows[color_idx],
                pair_field[color_idx],
                pair_value[color_idx],
                stacked_ext,
            )
    return (solution, forcing - coupled)


def sweep_kernel(dims, color, psrc, pfield, pval, forcing, mean, coef, outs, sides,
                 turn, shade, src_v, field_v, val_v, force_v, mean_v, ext, msg, allp, win, land, cbuf, faces,
                 inv, w2, r, sol, ready, diffs, spack, rpack, back, tail, local, send, recv, hsend, hrecv,
                 csend, crecv):
    batches, sources, modes, width, steps, cells, rows, fields, nz, owners, slabs = dims
    mode_dev = modes // owners
    per_batch = mode_dev // batches
    edge = width * steps
    core_cells = cells - 2 * edge
    slab_rows = core_cells // width
    cols = width - 2 * steps
    ny = cols * owners
    me = lax.axis_index("mode")
    slab = lax.axis_index("space")
    low, mid_at, high = pl.ds(0, edge), pl.ds(edge, core_cells), pl.ds(cells - edge, edge)
    has_low, has_high = slab > 0, slab < slabs - 1

    def peer(d):
        at = me
        bit = 1
        while bit < owners:
            if d & bit:
                at = at + bit * (1 - 2 * (me // bit % 2))
            bit *= 2
        return at

    far = range(owners - 1, 0, -1)

    barrier = pltpu.get_barrier_semaphore()
    for d in far:
        pl.semaphore_signal(
            barrier, inc=1, device_id={"mode": peer(d)}, device_id_type=pl.DeviceIdType.MESH
        )
    for there, at in ((has_low, slab - 1), (has_high, slab + 1)):

        @pl.when(there)
        def _():
            pl.semaphore_signal(
                barrier, inc=1, device_id={"space": at}, device_id_type=pl.DeviceIdType.MESH
            )

    def remote(src, dst, ssem, rsem, **where):
        return pltpu.make_async_remote_copy(
            src_ref=src, dst_ref=dst, send_sem=ssem, recv_sem=rsem, device_id=where,
            device_id_type=pl.DeviceIdType.MESH,
        )

    others = pl.ds(0, owners - 1)
    part_sems = (0, batches // 2, batches // 2 + batches, batches // 2 + 2 * batches)

    def pair_copy(q, d):
        return remote(
            msg.at[q], allp.at[q, me], send.at[0], recv.at[part_sems[0] + q], mode=peer(d)
        )

    def pairs_here(q):
        remote(
            allp.at[q, others], allp.at[q, others], send.at[0], recv.at[part_sems[0] + q],
            mode=peer(1),
        ).wait_recv()

    def value_copy(c, d):
        return remote(
            win.at[peer(d), c], land.at[c, me, :, mid_at], send.at[1], recv.at[part_sems[1] + c],
            mode=peer(d),
        )

    def values_here(c):
        remote(
            win.at[others, c], land.at[c, others, :, mid_at], send.at[1],
            recv.at[part_sems[1] + c], mode=peer(1),
        ).wait_recv()

    def up_copy(c):
        return remote(
            land.at[c, :, :, pl.ds(core_cells, edge)], land.at[c, :, :, low],
            hsend.at[0], hrecv.at[0, c], space=slab + 1,
        )

    def down_copy(c):
        return remote(
            land.at[c, :, :, pl.ds(edge, edge)], land.at[c, :, :, high],
            hsend.at[1], hrecv.at[1, c], space=slab - 1,
        )

    def coef_up():
        return remote(
            cbuf.at[:, pl.ds(core_cells, edge)], cbuf.at[:, low], csend.at[0], crecv.at[0],
            space=slab + 1,
        )

    def coef_down():
        return remote(
            cbuf.at[:, pl.ds(edge, edge)], cbuf.at[:, high], csend.at[1], crecv.at[1],
            space=slab - 1,
        )

    def solution_copy(c, d):
        return remote(
            spack.at[c, peer(d)], back.at[c, me], send.at[2], recv.at[part_sems[2] + c],
            mode=peer(d),
        )

    def residual_copy(n, d):
        return remote(
            rpack.at[n, peer(d)], tail.at[n, me], send.at[3], recv.at[part_sems[3] + n],
            mode=peer(d),
        )

    def solution_here(c):
        remote(
            spack.at[c, others], back.at[c, others], send.at[2], recv.at[part_sems[2] + c],
            mode=peer(1),
        ).wait_recv()

    def residual_here(n):
        remote(
            rpack.at[n, others], tail.at[n, others], send.at[3], recv.at[part_sems[3] + n],
            mode=peer(1),
        ).wait_recv()

    def all_sent():
        both = (allp.at[:, others], win.at[others], spack.at[:, others], rpack.at[:, others])
        for n, x in enumerate(both):
            remote(x, x, send.at[n], recv.at[0], mode=peer(1)).wait_send()
        for there, n, at in ((has_high, 0, slab + 1), (has_low, 1, slab - 1)):
            x = land.at[:, :, :, low]
            pl.when(there)(
                lambda: remote(x, x, hsend.at[n], hrecv.at[n, 0], space=at).wait_send()
            )

    loads = [
        pltpu.make_async_copy(src, dst, local.at[n])
        for n, (src, dst) in enumerate(
            (
                (color, shade), (psrc, src_v), (pfield, field_v), (pval, val_v),
                (forcing, force_v), (mean, mean_v),
            )
        )
    ]
    halves = ny // LANES
    for h in range(halves):
        part = pl.ds(h * LANES, LANES)
        loads.append(
            pltpu.make_async_copy(
                coef.at[:, part], ext.at[h, pl.ds(0, fields * slab_rows)], local.at[6 + h]
            )
        )
    for one in loads:
        one.start()

    for there, at in ((has_low, low), (has_high, high)):

        @pl.when(jnp.logical_not(there))
        def _():
            for c in range(batches):
                land[c, :, :, at] = jnp.zeros((owners, per_batch, edge), jnp.float32)
            cbuf[:, at] = jnp.zeros((cbuf.shape[0], edge), jnp.float32)

    r[...] = jnp.zeros_like(r)

    def earlier(shades, j):
        found = jnp.int32(0)
        for i in range(j):
            found = found | (shades[i] == shades[j]).astype(jnp.int32)
        return found

    loads[0].wait()
    second = []
    for o in range(owners):
        shades = [shade[o * mode_dev + j] for j in range(mode_dev)]
        second.append(
            functools.reduce(
                lambda x, y: x | y, [earlier(shades, j) << j for j in range(1, mode_dev)]
            )
        )
    shades = [shade[me * mode_dev + j] for j in range(mode_dev)]
    slots = [shades[j] * per_batch + earlier(shades, j) for j in range(mode_dev)]
    sub = lax.broadcasted_iota(jnp.int32, (mode_dev, ny), 0)
    holds = [sub == slots[j] for j in range(mode_dev)]

    def choose(masks, lines, shape):
        out = jnp.broadcast_to(lines[0], shape)
        for j in range(1, mode_dev):
            out = jnp.where(masks[j], jnp.broadcast_to(lines[j], shape), out)
        return out

    for n in (1, 2, 3):
        loads[n].wait()
    keys, vals = [], []
    for c in range(batches):
        src = src_v[c]
        owner = src >> 3
        bits = jnp.zeros_like(src)
        for o in range(owners):
            bits = jnp.where(owner == o, second[o], bits)
        source = owner * per_batch + ((bits >> (src & 7)) & 1)
        keys.append((field_v[c] * sources + source).astype(jnp.float32))
        vals.append(val_v[c])
    apart = batches // 2
    rest = jnp.zeros((mode_dev, LANES - batches * nz), jnp.float32)
    both = jnp.concatenate(
        [
            x
            for q in range(apart)
            for x in [keys[q], keys[q + apart], vals[q], vals[q + apart], rest]
        ],
        axis=1,
    )
    both = choose(
        [m[:, : apart * LANES] for m in holds], [both[j : j + 1] for j in range(mode_dev)],
        (mode_dev, apart * LANES),
    )
    for q in range(apart):
        for c in range(batches):
            one = both[c * per_batch : (c + 1) * per_batch, q * LANES : (q + 1) * LANES]
            msg[q, c] = one
            allp[q, me, c] = one

    loads[4].wait()
    lines = []
    for n in range(slab_rows):
        lines.append(
            choose(
                holds, [force_v[pl.ds(j * slab_rows + n, 1), :] for j in range(mode_dev)],
                (mode_dev, ny),
            )
        )
    blank = jnp.zeros((mode_dev, steps), jnp.float32)
    for p in range(owners):
        start, stop = p * cols - steps, (p + 1) * cols + steps
        parts = []
        for line in lines:
            if start < 0:
                parts.append(blank)
            parts.append(line[:, max(start, 0) : min(stop, ny)])
            if stop > ny:
                parts.append(blank)
        flat = jnp.concatenate(parts, axis=1)
        for c in range(batches):
            win[p, c] = flat[c * per_batch : (c + 1) * per_batch]

    beside = has_low.astype(jnp.int32) + has_high.astype(jnp.int32)
    pl.semaphore_wait(barrier, owners - 1 + beside)
    for d in far:
        value_copy(0, d).start()
    for d in far:
        pair_copy(0, d).start()
    for d in far:
        value_copy(1, d).start()
    for d in far:
        pair_copy(1, d).start()
    for c in range(2, batches):
        for d in far:
            value_copy(c, d).start()
    for c in range(batches):
        land[c, me, :, mid_at] = win[me, c]

    loads[5].wait()
    m = mean_v[...]
    place = lax.broadcasted_iota(jnp.int32, (slab_rows, ny), 1)
    level = lax.broadcasted_iota(jnp.int32, (slab_rows, ny), 0)
    right = jnp.where(place < ny - 1, pltpu.roll(m, ny - 1, 1), 0.0)
    left = jnp.where(place > 0, pltpu.roll(m, 1, 1), 0.0)
    after = jnp.where(level < slab_rows - 1, pltpu.roll(m, slab_rows - 1, 0), 0.0)
    before = jnp.where(level > 0, pltpu.roll(m, 1, 0), 0.0)
    for n, x in enumerate((m, 4.0 * m + right + left, before, after)):
        for h in range(halves):
            ext[h, pl.ds((fields + n) * slab_rows, slab_rows), :] = x[:, h * LANES : (h + 1) * LANES]
    for h in range(halves):
        loads[6 + h].wait()
    kpad = cbuf.shape[0]
    shift = lax.rem(ny - (me * cols - steps), ny)
    column = lax.broadcasted_iota(jnp.int32, (kpad, width), 1) + (me * cols - steps)
    real = (column >= 0) & (column < ny)
    parts = []
    for n in range(slab_rows):
        x = jnp.concatenate(
            [ext[h, pl.ds(n, kpad, stride=slab_rows), :] for h in range(halves)], axis=1
        )
        x = pltpu.roll(x, shift, 1)
        parts.append(jnp.where(real, x[:, :width], 0.0))
    cbuf[:, mid_at] = jnp.concatenate(parts, axis=1)
    pl.when(has_high)(lambda: coef_up().start())
    pl.when(has_low)(lambda: coef_down().start())

    def forward(c):
        values_here(c)
        pl.when(has_high)(lambda: up_copy(c).start())
        pl.when(has_low)(lambda: down_copy(c).start())

    pl.when(has_low)(lambda: coef_up().wait_recv())
    pl.when(has_high)(lambda: coef_down().wait_recv())
    a = cbuf[...]
    for n, hop in ((0, width), (2, 1)):
        face = 0.5 * (a + pltpu.roll(a, cells - hop, 1))
        faces[n] = face
        faces[n + 1] = pltpu.roll(face, hop, 1)
    centre, across = a[fields : fields + 1], a[fields + 1 : fields + 2]
    place = lax.broadcasted_iota(jnp.int32, (1, cells), 1)
    above = jnp.where(place < width, a[fields + 2 : fields + 3], pltpu.roll(centre, width, 1))
    below = jnp.where(
        place >= width * (rows - 1), a[fields + 3 : fields + 4],
        pltpu.roll(centre, cells - width, 1),
    )
    inside = across > 0.0
    diag = jnp.where(inside, 0.5 * (across + above + below), 1.0)
    inv[...] = jnp.where(inside, 1.0 / diag, 0.0)
    forward(0)
    tile = (8, LANES)
    level = lax.broadcasted_iota(jnp.int32, tile, 0).astype(jnp.float32)
    part = fields // 2
    def fill(q):
        pairs_here(q)
        every = jnp.concatenate(
            [allp[q, :, n].reshape(sources, LANES) for n in range(batches)], axis=0
        )
        turn[0] = jnp.concatenate([every, pltpu.roll(every, LANES - nz, 1)], axis=0).T
        code = turn[0, pl.ds(0, nz), :]
        turn[1, pl.ds(0, nz), :] = jnp.floor(code * (1.0 / sources))
        turn[2, pl.ds(0, nz), :] = code - sources * turn[1, pl.ds(0, nz), :]
        found = []
        for start in range(0, fields, part):
            sums = [[jnp.zeros(tile, jnp.float32)] * (sources // 8) for _ in range(part)]
            for z in range(nz):
                val, field, source = [
                    jnp.broadcast_to(turn[n, pl.ds(at, 1), :], tile)
                    for n, at in ((0, 2 * nz + z), (1, z), (2, z))
                ]
                picks = [
                    jnp.where(source == level + float(8 * h), val, 0.0)
                    for h in range(sources // 8)
                ]
                for f in range(part):
                    hit = jnp.where(field == float(start + f), 1.0, 0.0)
                    sums[f] = [x + hit * y for x, y in zip(sums[f], picks)]
            found += sums
        found = [x[h] for h in range(sources // 8) for x in found]
        found += [jnp.zeros(tile, jnp.float32)] * (w2.shape[2] // 8 - len(found))
        full = jnp.concatenate(found, axis=0).T
        hi = full.astype(jnp.bfloat16)
        mid = (full - hi.astype(jnp.float32)).astype(jnp.bfloat16)
        for h in range(2):
            c = q + h * (batches // 2)
            w2[c, pl.ds(0, modes), :] = hi[h * modes : (h + 1) * modes]
            w2[c, pl.ds(modes, modes), :] = mid[h * modes : (h + 1) * modes]

    fill(0)
    forward(1)

    def compact(x):
        return jnp.concatenate(
            [x[:, q * width + steps : q * width + steps + cols] for q in range(slab_rows)], axis=1
        )

    pieces = tail.shape[0]
    piece = slab_rows // pieces
    sent = 0

    def ship(n):
        start = edge + n * piece * width
        for b in range(batches):
            x = r[pl.ds(b * sources, sources), :]
            done = jnp.concatenate(
                [
                    x[:, start + q * width + steps : start + q * width + steps + cols]
                    for q in range(piece)
                ],
                axis=1,
            )
            for o in range(owners):
                rpack[n, o, b] = done[o * per_batch : (o + 1) * per_batch]
        for d in far:
            residual_copy(n, d).start()
        tail[n, me] = rpack[n, me]

    groups = cells // LANES

    def arrived(c):
        pl.when(has_low)(lambda: up_copy(c).wait_recv())
        pl.when(has_high)(lambda: down_copy(c).wait_recv())

    def scaled(k, g):
        at = pl.ds(g * LANES, LANES)
        mine = pl.ds(k % batches * sources, sources)
        x = r[mine, at]
        if k < batches:
            x = x + land[k, :, :, at].reshape(sources, LANES)
            r[mine, at] = x
        ready[:, pl.ds((g + 1) * LANES, LANES)] = x * inv[:, at]

    def differ(k, g):
        wide = ready[:, pl.ds(g * LANES, 3 * LANES)]
        here = wide[:, LANES : 2 * LANES]
        for n, hop in ((0, width), (2, 1)):
            ahead = pltpu.roll(wide, 3 * LANES - hop, 1)[:, LANES : 2 * LANES]
            behind = pltpu.roll(wide, hop, 1)[:, LANES : 2 * LANES]
            diffs[k % 2, n, :, pl.ds(g * LANES, LANES)] = here - ahead
            diffs[k % 2, n + 1, :, pl.ds(g * LANES, LANES)] = behind - here

    def prepare(k):
        for g in range(groups):
            scaled(k, g)
            if g:
                differ(k, g - 1)
        differ(k, groups - 1)

    ready[...] = jnp.zeros_like(ready)
    arrived(0)
    prepare(0)
    for k in range(steps):
        c = k % batches
        first = (width * (k + 1)) // LANES
        last = -(-(width * (rows - 1 - k)) // LANES)
        mine = pl.ds(c * sources, sources)
        if k == 1:
            forward(2)
            fill(1)
            forward(3)
        if k in (1, 2):
            arrived(k)
            prepare(k)
        if k == 2:
            arrived(3)
        inner = ready[:, pl.ds(LANES + edge, core_cells)]
        if k < batches:
            sol[mine, :] = inner
        else:
            done = compact(sol[mine, :] + inner)
            for o in range(owners):
                spack[c, o] = done[o * per_batch : (o + 1) * per_batch]
            for d in far:
                solution_copy(c, d).start()
            back[c, me] = spack[c, me]

        depth = pl.ds(0, fields * sources)
        for g in range(first, last, WIDE):
            w = LANES * min(WIDE, last - g)
            at = pl.ds(g * LANES, w)
            his, mids = [], []
            for h in range(sources // 8):
                near = [diffs[k % 2, n, pl.ds(h * 8, 8), at] for n in range(4)]
                for f in range(0, fields, 2):
                    pair = []
                    for e in (f, f + 1):
                        a = [jnp.broadcast_to(faces[n, pl.ds(e, 1), at], (8, w)) for n in range(4)]
                        pair.append((a[0] * near[0] - a[1] * near[1]) + (a[2] * near[2] - a[3] * near[3]))
                    p = jnp.concatenate(pair, axis=0)
                    hi = p.astype(jnp.bfloat16)
                    his.append(hi)
                    mids.append((p - hi.astype(jnp.float32)).astype(jnp.bfloat16))
            got = jnp.dot(
                w2[c, :, depth], jnp.concatenate(his, axis=0), preferred_element_type=jnp.float32
            )
            more = jnp.dot(
                w2[c, pl.ds(0, modes), depth], jnp.concatenate(mids, axis=0),
                preferred_element_type=jnp.float32,
            )
            r[:, at] = r[:, at] - (got[:modes] + got[modes:] + more)
            if 1 < k < steps - 1:
                for h in range(g, g + w // LANES):
                    scaled(k + 1, h)
                    if h > first:
                        differ(k + 1, h - 1)
                if g + WIDE >= last:
                    differ(k + 1, last - 1)
            if k == steps - 1:
                while sent < pieces and edge + (sent + 1) * piece * width <= (g + WIDE) * LANES:
                    ship(sent)
                    sent += 1

    row_slot = jnp.zeros((mode_dev, ny), jnp.int32)
    for j in range(mode_dev):
        row_slot = jnp.where(sub == j, slots[j], row_slot)
    gives = [row_slot == s for s in range(mode_dev)]

    def restore(out, got, start, count):
        for n in range(count):
            line = jnp.concatenate([x[:, n * cols : (n + 1) * cols] for x in got], axis=1)
            line = choose(gives, [line[s : s + 1] for s in range(mode_dev)], (mode_dev, ny))
            at = start + n
            for h in range(halves):
                row = (at // 8 * halves + h) * 8 + at % 8
                out[pl.ds(row, mode_dev, stride=slab_rows * halves), :] = line[
                    :, h * LANES : (h + 1) * LANES
                ]

    for c in range(batches):
        solution_here(c)
    got = [
        jnp.concatenate([back[c, p, :, : slab_rows * cols] for c in range(batches)], axis=0)
        for p in range(owners)
    ]
    restore(outs, got, 0, slab_rows)
    for n in range(pieces):
        residual_here(n)
        got = [tail[n, p].reshape(mode_dev, piece * cols) for p in range(owners)]
        restore(sides, got, n * piece, piece)
    all_sent()
    pl.when(has_high)(lambda: coef_up().wait_send())
    pl.when(has_low)(lambda: coef_down().wait_send())


def leave_kernel(outs, sides, first, second, sems):
    copies = [
        pltpu.make_async_copy(src, dst, sems.at[n])
        for n, (src, dst) in enumerate(((outs, first), (sides, second)))
    ]
    for one in copies:
        one.start()
    for one in copies:
        one.wait()


def patch_sizes(mesh, forcing, pair_src, coef_fields):
    owners = mesh.shape["mode"]
    slabs = mesh.shape["space"]
    modes, nx, ny = forcing.shape
    batches = pair_src.shape[0]
    nz = pair_src.shape[2]
    fields = coef_fields.shape[0]
    depth = SWEEPS * batches
    slab = nx // slabs
    cols = ny // owners
    width = cols + 2 * depth
    rows = slab + 2 * depth
    cells = rows * width
    sources = modes // batches
    fits = (
        slab > depth
        and cells % (2 * LANES) == 0
        and (slab * cols) % LANES == 0
        and (width * depth) % LANES == 0
        and width <= LANES
        and modes == 8 * owners
        and owners == 8
        and batches == 4
        and sources == 16
        and slab % 8 == 0
        and ny == 2 * LANES
        and fields <= 28
        and batches * nz <= LANES
    )
    return fits, (batches, sources, modes, width, depth, cells, rows, fields, nz, owners, slabs)


def by_patch(dims, forcing, mean_field, coef_fields, color, pair_src, pair_field, pair_value):
    batches, sources, modes, width, depth, cells, rows, fields, nz, owners, slabs = dims
    mode_dev, slab, ny = forcing.shape
    per_batch = mode_dev // batches
    cols = ny // owners
    core_cells = slab * width
    kpad = 32
    spread = -(-(fields * sources) // LANES) * LANES

    hbm = pl.BlockSpec(memory_space=pltpu.HBM)
    f32, i32 = jnp.float32, jnp.int32
    flat = pltpu.VMEM((mode_dev * slab * ny // LANES, LANES), f32)
    vmem = pl.BlockSpec(memory_space=pltpu.VMEM)
    sems = pltpu.SemaphoreType.DMA
    got = pl.pallas_call(
        functools.partial(sweep_kernel, dims),
        out_shape=(flat, flat),
        in_specs=[hbm] * 7,
        out_specs=(vmem, vmem),
        scratch_shapes=[
            pltpu.VMEM((3, LANES, LANES), f32),
            pltpu.SMEM((modes,), i32),
            pltpu.VMEM((batches, mode_dev, nz), i32),
            pltpu.VMEM((batches, mode_dev, nz), i32),
            pltpu.VMEM((batches, mode_dev, nz), f32),
            pltpu.VMEM((mode_dev * slab, ny), f32),
            pltpu.VMEM((slab, ny), f32),
            pltpu.VMEM((ny // LANES, kpad * slab, LANES), f32),
            pltpu.VMEM((batches // 2, batches, per_batch, LANES), f32),
            pltpu.VMEM((batches // 2, owners, batches, per_batch, LANES), f32),
            pltpu.VMEM((owners, batches, per_batch, core_cells), f32),
            pltpu.VMEM((batches, owners, per_batch, cells), f32),
            pltpu.VMEM((kpad, cells), f32),
            pltpu.VMEM((4, kpad, cells), f32),
            pltpu.VMEM((1, cells), f32),
            pltpu.VMEM((batches, 2 * modes, spread), jnp.bfloat16),
            pltpu.VMEM((modes, cells), f32),
            pltpu.VMEM((modes, core_cells), f32),
            pltpu.VMEM((sources, cells + 2 * LANES), f32),
            pltpu.VMEM((2, 4, sources, cells), f32),
            pltpu.VMEM((batches, owners, per_batch, slab * cols), f32),
            pltpu.VMEM((PIECES, owners, batches, per_batch, slab * cols // PIECES), f32),
            pltpu.VMEM((batches, owners, per_batch, slab * cols), f32),
            pltpu.VMEM((PIECES, owners, batches, per_batch, slab * cols // PIECES), f32),
            sems((8,)),
            sems((4,)),
            sems((batches // 2 + 2 * batches + PIECES,)),
            sems((2,)),
            sems((2, batches)),
            sems((2,)),
            sems((2,)),
        ],
        compiler_params=pltpu.CompilerParams(
            collective_id=0, has_side_effects=True
        ),
        name="sweeps",
    )(
        color, pair_src, pair_field, pair_value, forcing.reshape(mode_dev * slab, ny), mean_field,
        coef_fields.reshape(fields * slab, ny),
    )
    plain = jax.ShapeDtypeStruct((mode_dev * slab * ny // LANES, LANES), f32)
    got = pl.pallas_call(
        leave_kernel,
        out_shape=(plain, plain),
        in_specs=[pl.BlockSpec(memory_space=pltpu.VMEM)] * 2,
        out_specs=(pl.BlockSpec(memory_space=pl.ANY),) * 2,
        scratch_shapes=[sems((2,))],
        compiler_params=pltpu.CompilerParams(vmem_limit_bytes=4_000_000),
        name="leave",
    )(*got)
    shape = (mode_dev * slab // 8, ny // LANES, 8, LANES)
    return tuple(
        x.reshape(shape).transpose(0, 2, 1, 3).reshape(mode_dev, slab, ny) for x in got
    )


def solution(mesh):
    specs = (
        P("mode", "space", None),
        P("space", None),
        P(None, "space", None),
        P(),
        P(None, "mode", None),
        P(None, "mode", None),
        P(None, "mode", None),
    )

    def whole(*args):
        fits, dims = patch_sizes(mesh, args[0], args[4], args[2])
        body = functools.partial(by_patch, dims) if fits else by_batch
        return jax.shard_map(
            body,
            mesh=mesh,
            in_specs=specs,
            out_specs=(P("mode", "space", None), P("mode", "space", None)),
            check_vma=False,
        )(*args)

    return whole
```

```python
import functools

import jax
import jax.numpy as jnp
from jax import lax
from jax.experimental import pallas as pl
from jax.experimental.pallas import tpu as pltpu
from jax.sharding import PartitionSpec as P

SWEEPS = 2
LANES = 128
PIECES = 2
WIDE = 2


def with_halo(block, sides, width):
    for axis, dim in sides:
        count = lax.axis_size(axis)
        forward = [(i, i + 1) for i in range(count - 1)]
        backward = [(target, source) for source, target in forward]
        low = lax.ppermute(
            lax.slice_in_dim(block, block.shape[dim] - width, None, axis=dim), axis, forward
        )
        high = lax.ppermute(lax.slice_in_dim(block, 0, width, axis=dim), axis, backward)
        block = jnp.concatenate([low, block, high], axis=dim)
    return block


def stencil_ext(coeff_ext, value_ext):
    coeff_mid = coeff_ext[1:-1]
    value_mid = value_ext[1:-1]
    coeff_side = jnp.pad(coeff_mid, ((0, 0), (1, 1)))
    value_side = jnp.pad(value_mid, ((0, 0), (1, 1)))
    result = 0.5 * (coeff_mid + coeff_ext[2:]) * (value_mid - value_ext[2:])
    result = result + 0.5 * (coeff_mid + coeff_ext[:-2]) * (value_mid - value_ext[:-2])
    result = result + 0.5 * (coeff_mid + coeff_side[:, 2:]) * (value_mid - value_side[:, 2:])
    result = result + 0.5 * (coeff_mid + coeff_side[:, :-2]) * (value_mid - value_side[:, :-2])
    return result


def face_sum_ext(coeff_ext):
    coeff_mid = coeff_ext[1:-1]
    coeff_side = jnp.pad(coeff_mid, ((0, 0), (1, 1)))
    result = 0.5 * (coeff_mid + coeff_ext[2:])
    result = result + 0.5 * (coeff_mid + coeff_ext[:-2])
    result = result + 0.5 * (coeff_mid + coeff_side[:, 2:])
    result = result + 0.5 * (coeff_mid + coeff_side[:, :-2])
    return result


def couple(gathered, sources, field_ids, weights, stacked_ext):

    def reader(reader_entry):
        source_rows, field_rows, weight_rows = reader_entry
        values = jnp.take(gathered, source_rows, axis=0)
        coeffs = jnp.take(stacked_ext, field_rows + 1, axis=0)
        fluxes = jax.vmap(stencil_ext)(coeffs, values)
        return jnp.sum(weight_rows[:, None, None] * fluxes, axis=0)

    return lax.map(reader, (sources, field_ids, weights))


def ranks(color, mode_dev, batches):
    grouped = color.reshape(-1, mode_dev)
    onehot = (grouped[:, :, None] == jnp.arange(batches, dtype=jnp.int32)[None, None, :]).astype(
        jnp.int32
    )
    earlier = jnp.cumsum(onehot, axis=1) - onehot
    return jnp.sum(onehot * earlier, axis=2).reshape(-1)


def by_batch(forcing, mean_field, coef_fields, color, pair_src, pair_field, pair_value):
    mode_dev = forcing.shape[0]
    batches = pair_src.shape[0]
    per_batch = mode_dev // batches
    stacked = jnp.concatenate([mean_field[None], coef_fields], axis=0)
    stacked_ext = with_halo(stacked, (("space", 1),), 1)
    diag_sum = face_sum_ext(stacked_ext[0])
    ranking = ranks(color, mode_dev, batches)
    owners = jnp.arange(color.shape[0], dtype=jnp.int32) // mode_dev
    pool_rows = owners * per_batch + ranking
    source_rows = jnp.take(pool_rows, pair_src, axis=0)
    offset = lax.axis_index("mode") * mode_dev
    local_color = lax.dynamic_slice_in_dim(color, offset, mode_dev)
    local_rank = lax.dynamic_slice_in_dim(ranking, offset, mode_dev)
    positions = jnp.arange(mode_dev, dtype=jnp.int32)
    slot_numbers = jnp.arange(per_batch, dtype=jnp.int32)
    solution = jnp.zeros(forcing.shape, jnp.float32)
    coupled = jnp.zeros(forcing.shape, jnp.float32)
    for sweep_idx in range(SWEEPS):
        for color_idx in range(batches):
            active = local_color == color_idx
            update = jnp.where(active[:, None, None], (forcing - coupled) / diag_sum, 0.0)
            solution = solution + update
            selected = (active[None, :] & (local_rank[None, :] == slot_numbers[:, None])).astype(
                jnp.int32
            )
            chosen = jnp.sum(positions[None, :] * selected, axis=1)
            own_update = jnp.take(update, chosen, axis=0)
            inner = lax.all_gather(own_update, "mode", axis=0, tiled=True)
            gathered = with_halo(inner, (("space", 1),), 1)
            coupled = coupled + couple(
                gathered,
                source_rows[color_idx],
                pair_field[color_idx],
                pair_value[color_idx],
                stacked_ext,
            )
    return (solution, forcing - coupled)


def sweep_kernel(dims, color, psrc, pfield, pval, forcing, mean, coef, outs, sides,
                 turn, shade, src_v, field_v, val_v, force_v, mean_v, ext, msg, allp, win, land, cbuf, faces,
                 inv, w2, r, sol, ready, diffs, spack, rpack, back, tail, local, send, recv, hsend, hrecv,
                 csend, crecv):
    batches, sources, modes, width, steps, cells, rows, fields, nz, owners, slabs = dims
    mode_dev = modes // owners
    per_batch = mode_dev // batches
    edge = width * steps
    core_cells = cells - 2 * edge
    slab_rows = core_cells // width
    cols = width - 2 * steps
    ny = cols * owners
    me = lax.axis_index("mode")
    slab = lax.axis_index("space")
    low, mid_at, high = pl.ds(0, edge), pl.ds(edge, core_cells), pl.ds(cells - edge, edge)
    has_low, has_high = slab > 0, slab < slabs - 1

    def peer(d):
        at = me
        bit = 1
        while bit < owners:
            if d & bit:
                at = at + bit * (1 - 2 * (me // bit % 2))
            bit *= 2
        return at

    far = range(owners - 1, 0, -1)

    barrier = pltpu.get_barrier_semaphore()
    for d in far:
        pl.semaphore_signal(
            barrier, inc=1, device_id={"mode": peer(d)}, device_id_type=pl.DeviceIdType.MESH
        )
    for there, at in ((has_low, slab - 1), (has_high, slab + 1)):

        @pl.when(there)
        def _():
            pl.semaphore_signal(
                barrier, inc=1, device_id={"space": at}, device_id_type=pl.DeviceIdType.MESH
            )

    def remote(src, dst, ssem, rsem, **where):
        return pltpu.make_async_remote_copy(
            src_ref=src, dst_ref=dst, send_sem=ssem, recv_sem=rsem, device_id=where,
            device_id_type=pl.DeviceIdType.MESH,
        )

    others = pl.ds(0, owners - 1)
    part_sems = (0, batches // 2, batches // 2 + batches, batches // 2 + 2 * batches)

    def pair_copy(q, d):
        return remote(
            msg.at[q], allp.at[q, me], send.at[0], recv.at[part_sems[0] + q], mode=peer(d)
        )

    def pairs_here(q):
        remote(
            allp.at[q, others], allp.at[q, others], send.at[0], recv.at[part_sems[0] + q],
            mode=peer(1),
        ).wait_recv()

    def value_copy(c, d):
        return remote(
            win.at[peer(d), c], land.at[c, me, :, mid_at], send.at[1], recv.at[part_sems[1] + c],
            mode=peer(d),
        )

    def values_here(c):
        remote(
            win.at[others, c], land.at[c, others, :, mid_at], send.at[1],
            recv.at[part_sems[1] + c], mode=peer(1),
        ).wait_recv()

    def up_copy(c):
        return remote(
            land.at[c, :, :, pl.ds(core_cells, edge)], land.at[c, :, :, low],
            hsend.at[0], hrecv.at[0, c], space=slab + 1,
        )

    def down_copy(c):
        return remote(
            land.at[c, :, :, pl.ds(edge, edge)], land.at[c, :, :, high],
            hsend.at[1], hrecv.at[1, c], space=slab - 1,
        )

    def coef_up():
        return remote(
            cbuf.at[:, pl.ds(core_cells, edge)], cbuf.at[:, low], csend.at[0], crecv.at[0],
            space=slab + 1,
        )

    def coef_down():
        return remote(
            cbuf.at[:, pl.ds(edge, edge)], cbuf.at[:, high], csend.at[1], crecv.at[1],
            space=slab - 1,
        )

    def solution_copy(c, d):
        return remote(
            spack.at[c, peer(d)], back.at[c, me], send.at[2], recv.at[part_sems[2] + c],
            mode=peer(d),
        )

    def residual_copy(n, d):
        return remote(
            rpack.at[n, peer(d)], tail.at[n, me], send.at[3], recv.at[part_sems[3] + n],
            mode=peer(d),
        )

    def solution_here(c):
        remote(
            spack.at[c, others], back.at[c, others], send.at[2], recv.at[part_sems[2] + c],
            mode=peer(1),
        ).wait_recv()

    def residual_here(n):
        remote(
            rpack.at[n, others], tail.at[n, others], send.at[3], recv.at[part_sems[3] + n],
            mode=peer(1),
        ).wait_recv()

    def sent(n, x):
        remote(x, x, send.at[n], recv.at[0], mode=peer(1)).wait_send()

    def inputs_sent():
        sent(0, allp.at[:, others])
        sent(1, win.at[others])
        x = land.at[:, :, :, low]

        @pl.when(has_high)
        def _():
            remote(x, x, hsend.at[0], hrecv.at[0, 0], space=slab + 1).wait_send()
            coef_up().wait_send()

        @pl.when(has_low)
        def _():
            remote(x, x, hsend.at[1], hrecv.at[1, 0], space=slab - 1).wait_send()
            coef_down().wait_send()

    loads = [
        pltpu.make_async_copy(src, dst, local.at[n])
        for n, (src, dst) in enumerate(
            (
                (color, shade), (psrc, src_v), (pfield, field_v), (pval, val_v),
                (forcing, force_v), (mean, mean_v),
            )
        )
    ]
    halves = ny // LANES
    for h in range(halves):
        part = pl.ds(h * LANES, LANES)
        loads.append(
            pltpu.make_async_copy(
                coef.at[:, part], ext.at[h, pl.ds(0, fields * slab_rows)], local.at[6 + h]
            )
        )
    for one in loads:
        one.start()

    for there, at in ((has_low, low), (has_high, high)):

        @pl.when(jnp.logical_not(there))
        def _():
            for c in range(batches):
                land[c, :, :, at] = jnp.zeros((owners, per_batch, edge), jnp.float32)
            cbuf[:, at] = jnp.zeros((cbuf.shape[0], edge), jnp.float32)

    r[...] = jnp.zeros_like(r)

    def earlier(shades, j):
        found = jnp.int32(0)
        for i in range(j):
            found = found | (shades[i] == shades[j]).astype(jnp.int32)
        return found

    loads[0].wait()
    second = []
    for o in range(owners):
        shades = [shade[o * mode_dev + j] for j in range(mode_dev)]
        second.append(
            functools.reduce(
                lambda x, y: x | y, [earlier(shades, j) << j for j in range(1, mode_dev)]
            )
        )
    shades = [shade[me * mode_dev + j] for j in range(mode_dev)]
    slots = [shades[j] * per_batch + earlier(shades, j) for j in range(mode_dev)]
    sub = lax.broadcasted_iota(jnp.int32, (mode_dev, ny), 0)
    holds = [sub == slots[j] for j in range(mode_dev)]

    def choose(masks, lines, shape):
        out = jnp.broadcast_to(lines[0], shape)
        for j in range(1, mode_dev):
            out = jnp.where(masks[j], jnp.broadcast_to(lines[j], shape), out)
        return out

    for n in (1, 2, 3):
        loads[n].wait()
    keys, vals = [], []
    for c in range(batches):
        src = src_v[c]
        owner = src >> 3
        bits = jnp.zeros_like(src)
        for o in range(owners):
            bits = jnp.where(owner == o, second[o], bits)
        source = owner * per_batch + ((bits >> (src & 7)) & 1)
        keys.append((field_v[c] * sources + source).astype(jnp.float32))
        vals.append(val_v[c])
    apart = batches // 2
    rest = jnp.zeros((mode_dev, LANES - batches * nz), jnp.float32)
    both = jnp.concatenate(
        [
            x
            for q in range(apart)
            for x in [keys[q], keys[q + apart], vals[q], vals[q + apart], rest]
        ],
        axis=1,
    )
    both = choose(
        [m[:, : apart * LANES] for m in holds], [both[j : j + 1] for j in range(mode_dev)],
        (mode_dev, apart * LANES),
    )
    for q in range(apart):
        for c in range(batches):
            one = both[c * per_batch : (c + 1) * per_batch, q * LANES : (q + 1) * LANES]
            msg[q, c] = one
            allp[q, me, c] = one

    loads[4].wait()
    lines = []
    for n in range(slab_rows):
        lines.append(
            choose(
                holds, [force_v[pl.ds(j * slab_rows + n, 1), :] for j in range(mode_dev)],
                (mode_dev, ny),
            )
        )
    blank = jnp.zeros((mode_dev, steps), jnp.float32)
    for p in range(owners):
        start, stop = p * cols - steps, (p + 1) * cols + steps
        parts = []
        for line in lines:
            if start < 0:
                parts.append(blank)
            parts.append(line[:, max(start, 0) : min(stop, ny)])
            if stop > ny:
                parts.append(blank)
        flat = jnp.concatenate(parts, axis=1)
        for c in range(batches):
            win[p, c] = flat[c * per_batch : (c + 1) * per_batch]

    beside = has_low.astype(jnp.int32) + has_high.astype(jnp.int32)
    pl.semaphore_wait(barrier, owners - 1 + beside)
    for d in far:
        value_copy(0, d).start()
    for d in far:
        pair_copy(0, d).start()
    for d in far:
        value_copy(1, d).start()
    for d in far:
        pair_copy(1, d).start()
    for c in range(2, batches):
        for d in far:
            value_copy(c, d).start()
    for c in range(batches):
        land[c, me, :, mid_at] = win[me, c]

    loads[5].wait()
    m = mean_v[...]
    place = lax.broadcasted_iota(jnp.int32, (slab_rows, ny), 1)
    level = lax.broadcasted_iota(jnp.int32, (slab_rows, ny), 0)
    right = jnp.where(place < ny - 1, pltpu.roll(m, ny - 1, 1), 0.0)
    left = jnp.where(place > 0, pltpu.roll(m, 1, 1), 0.0)
    after = jnp.where(level < slab_rows - 1, pltpu.roll(m, slab_rows - 1, 0), 0.0)
    before = jnp.where(level > 0, pltpu.roll(m, 1, 0), 0.0)
    for n, x in enumerate((m, 4.0 * m + right + left, before, after)):
        for h in range(halves):
            ext[h, pl.ds((fields + n) * slab_rows, slab_rows), :] = x[:, h * LANES : (h + 1) * LANES]
    for h in range(halves):
        loads[6 + h].wait()
    kpad = cbuf.shape[0]
    shift = lax.rem(ny - (me * cols - steps), ny)
    column = lax.broadcasted_iota(jnp.int32, (kpad, width), 1) + (me * cols - steps)
    real = (column >= 0) & (column < ny)
    parts = []
    for n in range(slab_rows):
        x = jnp.concatenate(
            [ext[h, pl.ds(n, kpad, stride=slab_rows), :] for h in range(halves)], axis=1
        )
        x = pltpu.roll(x, shift, 1)
        parts.append(jnp.where(real, x[:, :width], 0.0))
    cbuf[:, mid_at] = jnp.concatenate(parts, axis=1)
    pl.when(has_high)(lambda: coef_up().start())
    pl.when(has_low)(lambda: coef_down().start())

    def forward(c):
        values_here(c)
        pl.when(has_high)(lambda: up_copy(c).start())
        pl.when(has_low)(lambda: down_copy(c).start())

    pl.when(has_low)(lambda: coef_up().wait_recv())
    pl.when(has_high)(lambda: coef_down().wait_recv())
    a = cbuf[...]
    for n, hop in ((0, width), (2, 1)):
        face = 0.5 * (a + pltpu.roll(a, cells - hop, 1))
        faces[n] = face
        faces[n + 1] = pltpu.roll(face, hop, 1)
    centre, across = a[fields : fields + 1], a[fields + 1 : fields + 2]
    place = lax.broadcasted_iota(jnp.int32, (1, cells), 1)
    above = jnp.where(place < width, a[fields + 2 : fields + 3], pltpu.roll(centre, width, 1))
    below = jnp.where(
        place >= width * (rows - 1), a[fields + 3 : fields + 4],
        pltpu.roll(centre, cells - width, 1),
    )
    inside = across > 0.0
    diag = jnp.where(inside, 0.5 * (across + above + below), 1.0)
    inv[...] = jnp.where(inside, 1.0 / diag, 0.0)
    forward(0)
    tile = (8, LANES)
    level = lax.broadcasted_iota(jnp.int32, tile, 0).astype(jnp.float32)
    part = fields // 2
    def fill(q):
        pairs_here(q)
        every = jnp.concatenate(
            [allp[q, :, n].reshape(sources, LANES) for n in range(batches)], axis=0
        )
        turn[0] = jnp.concatenate([every, pltpu.roll(every, LANES - nz, 1)], axis=0).T
        code = turn[0, pl.ds(0, nz), :]
        turn[1, pl.ds(0, nz), :] = jnp.floor(code * (1.0 / sources))
        turn[2, pl.ds(0, nz), :] = code - sources * turn[1, pl.ds(0, nz), :]
        found = []
        for start in range(0, fields, part):
            sums = [[jnp.zeros(tile, jnp.float32)] * (sources // 8) for _ in range(part)]
            for z in range(nz):
                val, field, source = [
                    jnp.broadcast_to(turn[n, pl.ds(at, 1), :], tile)
                    for n, at in ((0, 2 * nz + z), (1, z), (2, z))
                ]
                picks = [
                    jnp.where(source == level + float(8 * h), val, 0.0)
                    for h in range(sources // 8)
                ]
                for f in range(part):
                    hit = jnp.where(field == float(start + f), 1.0, 0.0)
                    sums[f] = [x + hit * y for x, y in zip(sums[f], picks)]
            found += sums
        found = [x[h] for h in range(sources // 8) for x in found]
        found += [jnp.zeros(tile, jnp.float32)] * (w2.shape[2] // 8 - len(found))
        full = jnp.concatenate(found, axis=0).T
        hi = full.astype(jnp.bfloat16)
        mid = (full - hi.astype(jnp.float32)).astype(jnp.bfloat16)
        for h in range(2):
            c = q + h * (batches // 2)
            w2[c, pl.ds(0, modes), :] = hi[h * modes : (h + 1) * modes]
            w2[c, pl.ds(modes, modes), :] = mid[h * modes : (h + 1) * modes]

    fill(0)
    forward(1)

    def compact(x):
        return jnp.concatenate(
            [x[:, q * width + steps : q * width + steps + cols] for q in range(slab_rows)], axis=1
        )

    pieces = tail.shape[0]
    piece = slab_rows // pieces
    shipped = 0

    def ship(n):
        start = edge + n * piece * width
        for b in range(batches):
            x = r[pl.ds(b * sources, sources), :]
            done = jnp.concatenate(
                [
                    x[:, start + q * width + steps : start + q * width + steps + cols]
                    for q in range(piece)
                ],
                axis=1,
            )
            for o in range(owners):
                rpack[n, o, b] = done[o * per_batch : (o + 1) * per_batch]
        for d in far:
            residual_copy(n, d).start()
        tail[n, me] = rpack[n, me]

    groups = cells // LANES

    def arrived(c):
        pl.when(has_low)(lambda: up_copy(c).wait_recv())
        pl.when(has_high)(lambda: down_copy(c).wait_recv())

    def scaled(k, g):
        at = pl.ds(g * LANES, LANES)
        mine = pl.ds(k % batches * sources, sources)
        x = r[mine, at]
        if k < batches:
            x = x + land[k, :, :, at].reshape(sources, LANES)
            r[mine, at] = x
        ready[:, pl.ds((g + 1) * LANES, LANES)] = x * inv[:, at]

    def differ(k, g):
        here = ready[:, pl.ds((g + 1) * LANES, LANES)]
        after = ready[:, pl.ds((g + 1) * LANES, 2 * LANES)]
        prior = ready[:, pl.ds(g * LANES, 2 * LANES)]
        at = pl.ds(g * LANES, LANES)
        for n, hop in ((0, width), (2, 1)):
            ahead = pltpu.roll(after, 2 * LANES - hop, 1)[:, :LANES]
            behind = pltpu.roll(prior, hop, 1)[:, LANES:]
            diffs[k % 2, n, :, at] = here - ahead
            diffs[k % 2, n + 1, :, at] = behind - here

    def prepare(k):
        for g in range(groups):
            scaled(k, g)
            if g:
                differ(k, g - 1)
        differ(k, groups - 1)

    ready[...] = jnp.zeros_like(ready)
    arrived(0)
    prepare(0)
    for k in range(steps):
        c = k % batches
        first = (width * (k + 1)) // LANES
        last = -(-(width * (rows - 1 - k)) // LANES)
        mine = pl.ds(c * sources, sources)
        if k == 1:
            forward(2)
            fill(1)
            forward(3)
        if k in (1, 2):
            arrived(k)
            prepare(k)
        if k == 2:
            arrived(3)
        inner = ready[:, pl.ds(LANES + edge, core_cells)]
        if k < batches:
            sol[mine, :] = inner
        else:
            done = compact(sol[mine, :] + inner)
            for o in range(owners):
                spack[c, o] = done[o * per_batch : (o + 1) * per_batch]
            for d in far:
                solution_copy(c, d).start()
            back[c, me] = spack[c, me]

        depth = pl.ds(0, fields * sources)
        chunks = []
        g = first
        while g < last:
            stop = last
            if k == steps - 1:
                step = piece * width // LANES
                stop = min(last, edge // LANES + ((g - edge // LANES) // step + 1) * step)
            chunks.append((g, LANES * min(WIDE, stop - g)))
            g += min(WIDE, stop - g)
        for g, w in chunks:
            at = pl.ds(g * LANES, w)
            his, mids = [], []
            for h in range(sources // 8):
                near = [diffs[k % 2, n, pl.ds(h * 8, 8), at] for n in range(4)]
                for f in range(0, fields, 2):
                    pair = []
                    for e in (f, f + 1):
                        a = [jnp.broadcast_to(faces[n, pl.ds(e, 1), at], (8, w)) for n in range(4)]
                        pair.append((a[0] * near[0] - a[1] * near[1]) + (a[2] * near[2] - a[3] * near[3]))
                    p = jnp.concatenate(pair, axis=0)
                    hi = p.astype(jnp.bfloat16)
                    his.append(hi)
                    mids.append((p - hi.astype(jnp.float32)).astype(jnp.bfloat16))
            got = jnp.dot(
                w2[c, :, depth], jnp.concatenate(his, axis=0), preferred_element_type=jnp.float32
            )
            more = jnp.dot(
                w2[c, pl.ds(0, modes), depth], jnp.concatenate(mids, axis=0),
                preferred_element_type=jnp.float32,
            )
            r[:, at] = r[:, at] - (got[:modes] + got[modes:] + more)
            if 1 < k < steps - 1:
                for h in range(g, g + w // LANES):
                    scaled(k + 1, h)
                    if h > first:
                        differ(k + 1, h - 1)
                if g + w // LANES >= last:
                    differ(k + 1, last - 1)
            if k == steps - 1:
                while shipped < pieces and edge + (shipped + 1) * piece * width <= g * LANES + w:
                    ship(shipped)
                    shipped += 1

    row_slot = jnp.zeros((mode_dev, ny), jnp.int32)
    for j in range(mode_dev):
        row_slot = jnp.where(sub == j, slots[j], row_slot)
    gives = [row_slot == s for s in range(mode_dev)]

    def restore(out, got, start, count):
        for n in range(count):
            line = jnp.concatenate([x[:, n * cols : (n + 1) * cols] for x in got], axis=1)
            line = choose(gives, [line[s : s + 1] for s in range(mode_dev)], (mode_dev, ny))
            at = start + n
            for h in range(halves):
                row = (at // 8 * halves + h) * 8 + at % 8
                out[pl.ds(row, mode_dev, stride=slab_rows * halves), :] = line[
                    :, h * LANES : (h + 1) * LANES
                ]

    inputs_sent()
    for c in range(batches):
        solution_here(c)
    got = [
        jnp.concatenate([back[c, p, :, : slab_rows * cols] for c in range(batches)], axis=0)
        for p in range(owners)
    ]
    restore(outs, got, 0, slab_rows)
    sent(2, spack.at[:, others])
    for n in range(pieces):
        residual_here(n)
        got = [tail[n, p].reshape(mode_dev, piece * cols) for p in range(owners)]
        restore(sides, got, n * piece, piece)
    sent(3, rpack.at[:, others])


def leave_kernel(outs, sides, first, second, sems):
    copies = [
        pltpu.make_async_copy(src, dst, sems.at[n])
        for n, (src, dst) in enumerate(((outs, first), (sides, second)))
    ]
    for one in copies:
        one.start()
    for one in copies:
        one.wait()


def patch_sizes(mesh, forcing, pair_src, coef_fields):
    owners = mesh.shape["mode"]
    slabs = mesh.shape["space"]
    modes, nx, ny = forcing.shape
    batches = pair_src.shape[0]
    nz = pair_src.shape[2]
    fields = coef_fields.shape[0]
    depth = SWEEPS * batches
    slab = nx // slabs
    cols = ny // owners
    width = cols + 2 * depth
    rows = slab + 2 * depth
    cells = rows * width
    sources = modes // batches
    fits = (
        slab > depth
        and cells % (2 * LANES) == 0
        and (slab * cols) % LANES == 0
        and (width * depth) % LANES == 0
        and width <= LANES
        and modes == 8 * owners
        and owners == 8
        and batches == 4
        and sources == 16
        and slab % 8 == 0
        and ny == 2 * LANES
        and fields <= 28
        and fields % 2 == 0
        and batches * nz <= LANES
    )
    return fits, (batches, sources, modes, width, depth, cells, rows, fields, nz, owners, slabs)


def by_patch(dims, forcing, mean_field, coef_fields, color, pair_src, pair_field, pair_value):
    batches, sources, modes, width, depth, cells, rows, fields, nz, owners, slabs = dims
    mode_dev, slab, ny = forcing.shape
    per_batch = mode_dev // batches
    cols = ny // owners
    core_cells = slab * width
    kpad = 32
    spread = -(-(fields * sources) // LANES) * LANES

    hbm = pl.BlockSpec(memory_space=pltpu.HBM)
    f32, i32 = jnp.float32, jnp.int32
    flat = pltpu.VMEM((mode_dev * slab * ny // LANES, LANES), f32)
    vmem = pl.BlockSpec(memory_space=pltpu.VMEM)
    sems = pltpu.SemaphoreType.DMA
    got = pl.pallas_call(
        functools.partial(sweep_kernel, dims),
        out_shape=(flat, flat),
        in_specs=[hbm] * 7,
        out_specs=(vmem, vmem),
        scratch_shapes=[
            pltpu.VMEM((3, LANES, LANES), f32),
            pltpu.SMEM((modes,), i32),
            pltpu.VMEM((batches, mode_dev, nz), i32),
            pltpu.VMEM((batches, mode_dev, nz), i32),
            pltpu.VMEM((batches, mode_dev, nz), f32),
            pltpu.VMEM((mode_dev * slab, ny), f32),
            pltpu.VMEM((slab, ny), f32),
            pltpu.VMEM((ny // LANES, kpad * slab, LANES), f32),
            pltpu.VMEM((batches // 2, batches, per_batch, LANES), f32),
            pltpu.VMEM((batches // 2, owners, batches, per_batch, LANES), f32),
            pltpu.VMEM((owners, batches, per_batch, core_cells), f32),
            pltpu.VMEM((batches, owners, per_batch, cells), f32),
            pltpu.VMEM((kpad, cells), f32),
            pltpu.VMEM((4, kpad, cells), f32),
            pltpu.VMEM((1, cells), f32),
            pltpu.VMEM((batches, 2 * modes, spread), jnp.bfloat16),
            pltpu.VMEM((modes, cells), f32),
            pltpu.VMEM((modes, core_cells), f32),
            pltpu.VMEM((sources, cells + 2 * LANES), f32),
            pltpu.VMEM((2, 4, sources, cells), f32),
            pltpu.VMEM((batches, owners, per_batch, slab * cols), f32),
            pltpu.VMEM((PIECES, owners, batches, per_batch, slab * cols // PIECES), f32),
            pltpu.VMEM((batches, owners, per_batch, slab * cols), f32),
            pltpu.VMEM((PIECES, owners, batches, per_batch, slab * cols // PIECES), f32),
            sems((8,)),
            sems((4,)),
            sems((batches // 2 + 2 * batches + PIECES,)),
            sems((2,)),
            sems((2, batches)),
            sems((2,)),
            sems((2,)),
        ],
        compiler_params=pltpu.CompilerParams(
            collective_id=0, has_side_effects=True
        ),
        name="sweeps",
    )(
        color, pair_src, pair_field, pair_value, forcing.reshape(mode_dev * slab, ny), mean_field,
        coef_fields.reshape(fields * slab, ny),
    )
    plain = jax.ShapeDtypeStruct((mode_dev * slab * ny // LANES, LANES), f32)
    got = pl.pallas_call(
        leave_kernel,
        out_shape=(plain, plain),
        in_specs=[pl.BlockSpec(memory_space=pltpu.VMEM)] * 2,
        out_specs=(pl.BlockSpec(memory_space=pl.ANY),) * 2,
        scratch_shapes=[sems((2,))],
        compiler_params=pltpu.CompilerParams(vmem_limit_bytes=4_000_000),
        name="leave",
    )(*got)
    shape = (mode_dev * slab // 8, ny // LANES, 8, LANES)
    return tuple(
        x.reshape(shape).transpose(0, 2, 1, 3).reshape(mode_dev, slab, ny) for x in got
    )


def solution(mesh):
    specs = (
        P("mode", "space", None),
        P("space", None),
        P(None, "space", None),
        P(),
        P(None, "mode", None),
        P(None, "mode", None),
        P(None, "mode", None),
    )

    def whole(*args):
        fits, dims = patch_sizes(mesh, args[0], args[4], args[2])
        body = functools.partial(by_patch, dims) if fits else by_batch
        return jax.shard_map(
            body,
            mesh=mesh,
            in_specs=specs,
            out_specs=(P("mode", "space", None), P("mode", "space", None)),
            check_vma=False,
        )(*args)

    return whole
```

```python
import functools

import jax
import jax.numpy as jnp
from jax import lax
from jax.experimental import pallas as pl
from jax.experimental.pallas import tpu as pltpu
from jax.sharding import PartitionSpec as P

SWEEPS = 2
LANES = 128
PIECES = 2
WIDE = 2


def with_halo(block, sides, width):
    for axis, dim in sides:
        count = lax.axis_size(axis)
        forward = [(i, i + 1) for i in range(count - 1)]
        backward = [(target, source) for source, target in forward]
        low = lax.ppermute(
            lax.slice_in_dim(block, block.shape[dim] - width, None, axis=dim), axis, forward
        )
        high = lax.ppermute(lax.slice_in_dim(block, 0, width, axis=dim), axis, backward)
        block = jnp.concatenate([low, block, high], axis=dim)
    return block


def stencil_ext(coeff_ext, value_ext):
    coeff_mid = coeff_ext[1:-1]
    value_mid = value_ext[1:-1]
    coeff_side = jnp.pad(coeff_mid, ((0, 0), (1, 1)))
    value_side = jnp.pad(value_mid, ((0, 0), (1, 1)))
    result = 0.5 * (coeff_mid + coeff_ext[2:]) * (value_mid - value_ext[2:])
    result = result + 0.5 * (coeff_mid + coeff_ext[:-2]) * (value_mid - value_ext[:-2])
    result = result + 0.5 * (coeff_mid + coeff_side[:, 2:]) * (value_mid - value_side[:, 2:])
    result = result + 0.5 * (coeff_mid + coeff_side[:, :-2]) * (value_mid - value_side[:, :-2])
    return result


def face_sum_ext(coeff_ext):
    coeff_mid = coeff_ext[1:-1]
    coeff_side = jnp.pad(coeff_mid, ((0, 0), (1, 1)))
    result = 0.5 * (coeff_mid + coeff_ext[2:])
    result = result + 0.5 * (coeff_mid + coeff_ext[:-2])
    result = result + 0.5 * (coeff_mid + coeff_side[:, 2:])
    result = result + 0.5 * (coeff_mid + coeff_side[:, :-2])
    return result


def couple(gathered, sources, field_ids, weights, stacked_ext):

    def reader(reader_entry):
        source_rows, field_rows, weight_rows = reader_entry
        values = jnp.take(gathered, source_rows, axis=0)
        coeffs = jnp.take(stacked_ext, field_rows + 1, axis=0)
        fluxes = jax.vmap(stencil_ext)(coeffs, values)
        return jnp.sum(weight_rows[:, None, None] * fluxes, axis=0)

    return lax.map(reader, (sources, field_ids, weights))


def ranks(color, mode_dev, batches):
    grouped = color.reshape(-1, mode_dev)
    onehot = (grouped[:, :, None] == jnp.arange(batches, dtype=jnp.int32)[None, None, :]).astype(
        jnp.int32
    )
    earlier = jnp.cumsum(onehot, axis=1) - onehot
    return jnp.sum(onehot * earlier, axis=2).reshape(-1)


def by_batch(forcing, mean_field, coef_fields, color, pair_src, pair_field, pair_value):
    mode_dev = forcing.shape[0]
    batches = pair_src.shape[0]
    per_batch = mode_dev // batches
    stacked = jnp.concatenate([mean_field[None], coef_fields], axis=0)
    stacked_ext = with_halo(stacked, (("space", 1),), 1)
    diag_sum = face_sum_ext(stacked_ext[0])
    ranking = ranks(color, mode_dev, batches)
    owners = jnp.arange(color.shape[0], dtype=jnp.int32) // mode_dev
    pool_rows = owners * per_batch + ranking
    source_rows = jnp.take(pool_rows, pair_src, axis=0)
    offset = lax.axis_index("mode") * mode_dev
    local_color = lax.dynamic_slice_in_dim(color, offset, mode_dev)
    local_rank = lax.dynamic_slice_in_dim(ranking, offset, mode_dev)
    positions = jnp.arange(mode_dev, dtype=jnp.int32)
    slot_numbers = jnp.arange(per_batch, dtype=jnp.int32)
    solution = jnp.zeros(forcing.shape, jnp.float32)
    coupled = jnp.zeros(forcing.shape, jnp.float32)
    for sweep_idx in range(SWEEPS):
        for color_idx in range(batches):
            active = local_color == color_idx
            update = jnp.where(active[:, None, None], (forcing - coupled) / diag_sum, 0.0)
            solution = solution + update
            selected = (active[None, :] & (local_rank[None, :] == slot_numbers[:, None])).astype(
                jnp.int32
            )
            chosen = jnp.sum(positions[None, :] * selected, axis=1)
            own_update = jnp.take(update, chosen, axis=0)
            inner = lax.all_gather(own_update, "mode", axis=0, tiled=True)
            gathered = with_halo(inner, (("space", 1),), 1)
            coupled = coupled + couple(
                gathered,
                source_rows[color_idx],
                pair_field[color_idx],
                pair_value[color_idx],
                stacked_ext,
            )
    return (solution, forcing - coupled)


def sweep_kernel(dims, color, psrc, pfield, pval, forcing, mean, coef, outs, sides,
                 turn, shade, src_v, field_v, val_v, force_v, mean_v, ext, msg, allp, win, land, cbuf, faces,
                 inv, w2, r, sol, ready, diffs, spack, rpack, back, tail, local, send, recv, hsend, hrecv,
                 csend, crecv):
    batches, sources, modes, width, steps, cells, rows, fields, nz, owners, slabs = dims
    mode_dev = modes // owners
    per_batch = mode_dev // batches
    edge = width * steps
    core_cells = cells - 2 * edge
    slab_rows = core_cells // width
    cols = width - 2 * steps
    ny = cols * owners
    me = lax.axis_index("mode")
    slab = lax.axis_index("space")
    low, mid_at, high = pl.ds(0, edge), pl.ds(edge, core_cells), pl.ds(cells - edge, edge)
    has_low, has_high = slab > 0, slab < slabs - 1

    def peer(d):
        at = me
        bit = 1
        while bit < owners:
            if d & bit:
                at = at + bit * (1 - 2 * (me // bit % 2))
            bit *= 2
        return at

    far = range(owners - 1, 0, -1)

    barrier = pltpu.get_barrier_semaphore()
    for d in far:
        pl.semaphore_signal(
            barrier, inc=1, device_id={"mode": peer(d)}, device_id_type=pl.DeviceIdType.MESH
        )
    for there, at in ((has_low, slab - 1), (has_high, slab + 1)):

        @pl.when(there)
        def _():
            pl.semaphore_signal(
                barrier, inc=1, device_id={"space": at}, device_id_type=pl.DeviceIdType.MESH
            )

    def remote(src, dst, ssem, rsem, **where):
        return pltpu.make_async_remote_copy(
            src_ref=src, dst_ref=dst, send_sem=ssem, recv_sem=rsem, device_id=where,
            device_id_type=pl.DeviceIdType.MESH,
        )

    others = pl.ds(0, owners - 1)
    part_sems = (0, batches // 2, batches // 2 + batches, batches // 2 + 2 * batches)

    def pair_copy(q, d):
        return remote(
            msg.at[q], allp.at[q, me], send.at[0], recv.at[part_sems[0] + q], mode=peer(d)
        )

    def pairs_here(q):
        remote(
            allp.at[q, others], allp.at[q, others], send.at[0], recv.at[part_sems[0] + q],
            mode=peer(1),
        ).wait_recv()

    def value_copy(c, d):
        return remote(
            win.at[peer(d), c], land.at[c, me, :, mid_at], send.at[1], recv.at[part_sems[1] + c],
            mode=peer(d),
        )

    def values_here(c):
        remote(
            win.at[others, c], land.at[c, others, :, mid_at], send.at[1],
            recv.at[part_sems[1] + c], mode=peer(1),
        ).wait_recv()

    def up_copy(c):
        return remote(
            land.at[c, :, :, pl.ds(core_cells, edge)], land.at[c, :, :, low],
            hsend.at[0], hrecv.at[0, c], space=slab + 1,
        )

    def down_copy(c):
        return remote(
            land.at[c, :, :, pl.ds(edge, edge)], land.at[c, :, :, high],
            hsend.at[1], hrecv.at[1, c], space=slab - 1,
        )

    def coef_up():
        return remote(
            cbuf.at[:, pl.ds(core_cells, edge)], cbuf.at[:, low], csend.at[0], crecv.at[0],
            space=slab + 1,
        )

    def coef_down():
        return remote(
            cbuf.at[:, pl.ds(edge, edge)], cbuf.at[:, high], csend.at[1], crecv.at[1],
            space=slab - 1,
        )

    def solution_copy(c, d):
        return remote(
            spack.at[c, peer(d)], back.at[c, me], send.at[2], recv.at[part_sems[2] + c],
            mode=peer(d),
        )

    def residual_copy(n, d):
        return remote(
            rpack.at[n, peer(d)], tail.at[n, me], send.at[3], recv.at[part_sems[3] + n],
            mode=peer(d),
        )

    def solution_here(c):
        remote(
            spack.at[c, others], back.at[c, others], send.at[2], recv.at[part_sems[2] + c],
            mode=peer(1),
        ).wait_recv()

    def residual_here(n):
        remote(
            rpack.at[n, others], tail.at[n, others], send.at[3], recv.at[part_sems[3] + n],
            mode=peer(1),
        ).wait_recv()

    def sent(n, x):
        remote(x, x, send.at[n], recv.at[0], mode=peer(1)).wait_send()

    def inputs_sent():
        sent(0, allp.at[:, others])
        sent(1, win.at[others])
        x = land.at[:, :, :, low]

        @pl.when(has_high)
        def _():
            remote(x, x, hsend.at[0], hrecv.at[0, 0], space=slab + 1).wait_send()
            coef_up().wait_send()

        @pl.when(has_low)
        def _():
            remote(x, x, hsend.at[1], hrecv.at[1, 0], space=slab - 1).wait_send()
            coef_down().wait_send()

    loads = [
        pltpu.make_async_copy(src, dst, local.at[n])
        for n, (src, dst) in enumerate(
            (
                (color, shade), (psrc, src_v), (pfield, field_v), (pval, val_v),
                (forcing, force_v), (mean, mean_v),
            )
        )
    ]
    halves = ny // LANES
    for h in range(halves):
        part = pl.ds(h * LANES, LANES)
        loads.append(
            pltpu.make_async_copy(
                coef.at[:, part], ext.at[h, pl.ds(0, fields * slab_rows)], local.at[6 + h]
            )
        )
    for one in loads:
        one.start()

    for there, at in ((has_low, low), (has_high, high)):

        @pl.when(jnp.logical_not(there))
        def _():
            for c in range(batches):
                land[c, :, :, at] = jnp.zeros((owners, per_batch, edge), jnp.float32)
            cbuf[:, at] = jnp.zeros((cbuf.shape[0], edge), jnp.float32)

    r[...] = jnp.zeros_like(r)

    def earlier(shades, j):
        found = jnp.int32(0)
        for i in range(j):
            found = found | (shades[i] == shades[j]).astype(jnp.int32)
        return found

    loads[0].wait()
    second = []
    for o in range(owners):
        shades = [shade[o * mode_dev + j] for j in range(mode_dev)]
        second.append(
            functools.reduce(
                lambda x, y: x | y, [earlier(shades, j) << j for j in range(1, mode_dev)]
            )
        )
    shades = [shade[me * mode_dev + j] for j in range(mode_dev)]
    slots = [shades[j] * per_batch + earlier(shades, j) for j in range(mode_dev)]
    sub = lax.broadcasted_iota(jnp.int32, (mode_dev, ny), 0)
    holds = [sub == slots[j] for j in range(mode_dev)]

    def choose(masks, lines, shape):
        out = jnp.broadcast_to(lines[0], shape)
        for j in range(1, mode_dev):
            out = jnp.where(masks[j], jnp.broadcast_to(lines[j], shape), out)
        return out

    for n in (1, 2, 3):
        loads[n].wait()
    keys, vals = [], []
    for c in range(batches):
        src = src_v[c]
        owner = src >> 3
        bits = jnp.zeros_like(src)
        for o in range(owners):
            bits = jnp.where(owner == o, second[o], bits)
        source = owner * per_batch + ((bits >> (src & 7)) & 1)
        keys.append((field_v[c] * sources + source).astype(jnp.float32))
        vals.append(val_v[c])
    apart = batches // 2
    rest = jnp.zeros((mode_dev, LANES - batches * nz), jnp.float32)
    both = jnp.concatenate(
        [
            x
            for q in range(apart)
            for x in [keys[q], keys[q + apart], vals[q], vals[q + apart], rest]
        ],
        axis=1,
    )
    both = choose(
        [m[:, : apart * LANES] for m in holds], [both[j : j + 1] for j in range(mode_dev)],
        (mode_dev, apart * LANES),
    )
    for q in range(apart):
        for c in range(batches):
            one = both[c * per_batch : (c + 1) * per_batch, q * LANES : (q + 1) * LANES]
            msg[q, c] = one
            allp[q, me, c] = one

    loads[4].wait()
    lines = []
    for n in range(slab_rows):
        lines.append(
            choose(
                holds, [force_v[pl.ds(j * slab_rows + n, 1), :] for j in range(mode_dev)],
                (mode_dev, ny),
            )
        )
    blank = jnp.zeros((mode_dev, steps), jnp.float32)
    for p in range(owners):
        start, stop = p * cols - steps, (p + 1) * cols + steps
        parts = []
        for line in lines:
            if start < 0:
                parts.append(blank)
            parts.append(line[:, max(start, 0) : min(stop, ny)])
            if stop > ny:
                parts.append(blank)
        flat = jnp.concatenate(parts, axis=1)
        for c in range(batches):
            win[p, c] = flat[c * per_batch : (c + 1) * per_batch]

    beside = has_low.astype(jnp.int32) + has_high.astype(jnp.int32)
    pl.semaphore_wait(barrier, owners - 1 + beside)
    for d in far:
        value_copy(0, d).start()
    for d in far:
        pair_copy(0, d).start()
    for d in far:
        value_copy(1, d).start()
    for d in far:
        pair_copy(1, d).start()
    for c in range(2, batches):
        for d in far:
            value_copy(c, d).start()
    for c in range(batches):
        land[c, me, :, mid_at] = win[me, c]

    loads[5].wait()
    m = mean_v[...]
    place = lax.broadcasted_iota(jnp.int32, (slab_rows, ny), 1)
    level = lax.broadcasted_iota(jnp.int32, (slab_rows, ny), 0)
    right = jnp.where(place < ny - 1, pltpu.roll(m, ny - 1, 1), 0.0)
    left = jnp.where(place > 0, pltpu.roll(m, 1, 1), 0.0)
    after = jnp.where(level < slab_rows - 1, pltpu.roll(m, slab_rows - 1, 0), 0.0)
    before = jnp.where(level > 0, pltpu.roll(m, 1, 0), 0.0)
    for n, x in enumerate((m, 4.0 * m + right + left, before, after)):
        for h in range(halves):
            ext[h, pl.ds((fields + n) * slab_rows, slab_rows), :] = x[:, h * LANES : (h + 1) * LANES]
    for h in range(halves):
        loads[6 + h].wait()
    kpad = cbuf.shape[0]
    shift = lax.rem(ny - (me * cols - steps), ny)
    column = lax.broadcasted_iota(jnp.int32, (kpad, width), 1) + (me * cols - steps)
    real = (column >= 0) & (column < ny)
    parts = []
    for n in range(slab_rows):
        x = jnp.concatenate(
            [ext[h, pl.ds(n, kpad, stride=slab_rows), :] for h in range(halves)], axis=1
        )
        x = pltpu.roll(x, shift, 1)
        parts.append(jnp.where(real, x[:, :width], 0.0))
    cbuf[:, mid_at] = jnp.concatenate(parts, axis=1)
    pl.when(has_high)(lambda: coef_up().start())
    pl.when(has_low)(lambda: coef_down().start())

    def forward(c):
        values_here(c)
        pl.when(has_high)(lambda: up_copy(c).start())
        pl.when(has_low)(lambda: down_copy(c).start())

    pl.when(has_low)(lambda: coef_up().wait_recv())
    pl.when(has_high)(lambda: coef_down().wait_recv())
    a = cbuf[...]
    for n, hop in ((0, width), (2, 1)):
        face = 0.5 * (a + pltpu.roll(a, cells - hop, 1))
        faces[n] = face
        faces[n + 1] = pltpu.roll(face, hop, 1)
    centre, across = a[fields : fields + 1], a[fields + 1 : fields + 2]
    place = lax.broadcasted_iota(jnp.int32, (1, cells), 1)
    above = jnp.where(place < width, a[fields + 2 : fields + 3], pltpu.roll(centre, width, 1))
    below = jnp.where(
        place >= width * (rows - 1), a[fields + 3 : fields + 4],
        pltpu.roll(centre, cells - width, 1),
    )
    inside = across > 0.0
    diag = jnp.where(inside, 0.5 * (across + above + below), 1.0)
    inv[...] = jnp.where(inside, 1.0 / diag, 0.0)
    forward(0)
    tile = (8, LANES)
    level = lax.broadcasted_iota(jnp.int32, tile, 0).astype(jnp.float32)
    part = fields // 2
    def fill(q):
        pairs_here(q)
        every = jnp.concatenate(
            [allp[q, :, n].reshape(sources, LANES) for n in range(batches)], axis=0
        )
        turn[0] = jnp.concatenate([every, pltpu.roll(every, LANES - nz, 1)], axis=0).T
        code = turn[0, pl.ds(0, nz), :]
        turn[1, pl.ds(0, nz), :] = jnp.floor(code * (1.0 / sources))
        turn[2, pl.ds(0, nz), :] = code - sources * turn[1, pl.ds(0, nz), :]
        found = []
        for start in range(0, fields, part):
            sums = [[jnp.zeros(tile, jnp.float32)] * (sources // 8) for _ in range(part)]
            for z in range(nz):
                val, field, source = [
                    jnp.broadcast_to(turn[n, pl.ds(at, 1), :], tile)
                    for n, at in ((0, 2 * nz + z), (1, z), (2, z))
                ]
                picks = [
                    jnp.where(source == level + float(8 * h), val, 0.0)
                    for h in range(sources // 8)
                ]
                for f in range(part):
                    hit = jnp.where(field == float(start + f), 1.0, 0.0)
                    sums[f] = [x + hit * y for x, y in zip(sums[f], picks)]
            found += sums
        found = [x[h] for h in range(sources // 8) for x in found]
        found += [jnp.zeros(tile, jnp.float32)] * (w2.shape[2] // 8 - len(found))
        full = jnp.concatenate(found, axis=0).T
        hi = full.astype(jnp.bfloat16)
        mid = (full - hi.astype(jnp.float32)).astype(jnp.bfloat16)
        for h in range(2):
            c = q + h * (batches // 2)
            w2[c, pl.ds(0, modes), :] = hi[h * modes : (h + 1) * modes]
            w2[c, pl.ds(modes, modes), :] = mid[h * modes : (h + 1) * modes]

    fill(0)
    forward(1)

    def compact(x):
        return jnp.concatenate(
            [x[:, q * width + steps : q * width + steps + cols] for q in range(slab_rows)], axis=1
        )

    pieces = tail.shape[0]
    piece = slab_rows // pieces
    shipped = 0

    def ship(n):
        start = edge + n * piece * width
        for b in range(batches):
            x = r[pl.ds(b * sources, sources), :]
            done = jnp.concatenate(
                [
                    x[:, start + q * width + steps : start + q * width + steps + cols]
                    for q in range(piece)
                ],
                axis=1,
            )
            for o in range(owners):
                rpack[n, o, b] = done[o * per_batch : (o + 1) * per_batch]
        for d in far:
            residual_copy(n, d).start()
        tail[n, me] = rpack[n, me]

    groups = cells // LANES

    def arrived(c):
        pl.when(has_low)(lambda: up_copy(c).wait_recv())
        pl.when(has_high)(lambda: down_copy(c).wait_recv())

    def scaled(k, g):
        at = pl.ds(g * LANES, LANES)
        mine = pl.ds(k % batches * sources, sources)
        x = r[mine, at]
        if k < batches:
            x = x + land[k, :, :, at].reshape(sources, LANES)
            r[mine, at] = x
        ready[:, pl.ds((g + 1) * LANES, LANES)] = x * inv[:, at]

    def differ(k, g):
        here = ready[:, pl.ds((g + 1) * LANES, LANES)]
        after = ready[:, pl.ds((g + 1) * LANES, 2 * LANES)]
        prior = ready[:, pl.ds(g * LANES, 2 * LANES)]
        at = pl.ds(g * LANES, LANES)
        for n, hop in ((0, width), (2, 1)):
            ahead = pltpu.roll(after, 2 * LANES - hop, 1)[:, :LANES]
            behind = pltpu.roll(prior, hop, 1)[:, LANES:]
            diffs[k % 2, n, :, at] = here - ahead
            diffs[k % 2, n + 1, :, at] = behind - here

    def prepare(k):
        mine = pl.ds(k * sources, sources)
        x = r[mine, :] + land[k].reshape(sources, cells)
        r[mine, :] = x
        u = x * inv[...]
        ready[:, pl.ds(LANES, cells)] = u
        for n, hop in ((0, width), (2, 1)):
            diffs[k % 2, n] = u - pltpu.roll(u, cells - hop, 1)
            diffs[k % 2, n + 1] = pltpu.roll(u, hop, 1) - u

    ready[...] = jnp.zeros_like(ready)
    arrived(0)
    prepare(0)
    for k in range(steps):
        c = k % batches
        first = (width * (k + 1)) // LANES
        last = -(-(width * (rows - 1 - k)) // LANES)
        mine = pl.ds(c * sources, sources)
        if k == 1:
            forward(2)
            fill(1)
            forward(3)
        if k in (1, 2):
            arrived(k)
            prepare(k)
        if k == 2:
            arrived(3)
        inner = ready[:, pl.ds(LANES + edge, core_cells)]
        if k < batches:
            sol[mine, :] = inner
        else:
            done = compact(sol[mine, :] + inner)
            for o in range(owners):
                spack[c, o] = done[o * per_batch : (o + 1) * per_batch]
            for d in far:
                solution_copy(c, d).start()
            back[c, me] = spack[c, me]

        depth = pl.ds(0, fields * sources)
        chunks = []
        g = first
        while g < last:
            stop = last
            if k == steps - 1:
                step = piece * width // LANES
                stop = min(last, edge // LANES + ((g - edge // LANES) // step + 1) * step)
            chunks.append((g, LANES * min(WIDE, stop - g)))
            g += min(WIDE, stop - g)
        for g, w in chunks:
            at = pl.ds(g * LANES, w)
            his, mids = [], []
            for h in range(sources // 8):
                near = [diffs[k % 2, n, pl.ds(h * 8, 8), at] for n in range(4)]
                for f in range(0, fields, 2):
                    pair = []
                    for e in (f, f + 1):
                        a = [jnp.broadcast_to(faces[n, pl.ds(e, 1), at], (8, w)) for n in range(4)]
                        pair.append((a[0] * near[0] - a[1] * near[1]) + (a[2] * near[2] - a[3] * near[3]))
                    p = jnp.concatenate(pair, axis=0)
                    hi = p.astype(jnp.bfloat16)
                    his.append(hi)
                    mids.append((p - hi.astype(jnp.float32)).astype(jnp.bfloat16))
            got = jnp.dot(
                w2[c, :, depth], jnp.concatenate(his, axis=0), preferred_element_type=jnp.float32
            )
            more = jnp.dot(
                w2[c, pl.ds(0, modes), depth], jnp.concatenate(mids, axis=0),
                preferred_element_type=jnp.float32,
            )
            r[:, at] = r[:, at] - (got[:modes] + got[modes:] + more)
            if 1 < k < steps - 1:
                for h in range(g, g + w // LANES):
                    scaled(k + 1, h)
                    if h > first:
                        differ(k + 1, h - 1)
                if g + w // LANES >= last:
                    differ(k + 1, last - 1)
            if k == steps - 1:
                while shipped < pieces and edge + (shipped + 1) * piece * width <= g * LANES + w:
                    ship(shipped)
                    shipped += 1

    row_slot = jnp.zeros((mode_dev, ny), jnp.int32)
    for j in range(mode_dev):
        row_slot = jnp.where(sub == j, slots[j], row_slot)
    gives = [row_slot == s for s in range(mode_dev)]

    def restore(out, got, start, count):
        for n in range(count):
            line = jnp.concatenate([x[:, n * cols : (n + 1) * cols] for x in got], axis=1)
            line = choose(gives, [line[s : s + 1] for s in range(mode_dev)], (mode_dev, ny))
            at = start + n
            for h in range(halves):
                row = (at // 8 * halves + h) * 8 + at % 8
                out[pl.ds(row, mode_dev, stride=slab_rows * halves), :] = line[
                    :, h * LANES : (h + 1) * LANES
                ]

    inputs_sent()
    for c in range(batches):
        solution_here(c)
    got = [
        jnp.concatenate([back[c, p, :, : slab_rows * cols] for c in range(batches)], axis=0)
        for p in range(owners)
    ]
    restore(outs, got, 0, slab_rows)
    sent(2, spack.at[:, others])
    for n in range(pieces):
        residual_here(n)
        got = [tail[n, p].reshape(mode_dev, piece * cols) for p in range(owners)]
        restore(sides, got, n * piece, piece)
    sent(3, rpack.at[:, others])


def leave_kernel(outs, sides, first, second, sems):
    copies = [
        pltpu.make_async_copy(src, dst, sems.at[n])
        for n, (src, dst) in enumerate(((outs, first), (sides, second)))
    ]
    for one in copies:
        one.start()
    for one in copies:
        one.wait()


def patch_sizes(mesh, forcing, pair_src, coef_fields):
    owners = mesh.shape["mode"]
    slabs = mesh.shape["space"]
    modes, nx, ny = forcing.shape
    batches = pair_src.shape[0]
    nz = pair_src.shape[2]
    fields = coef_fields.shape[0]
    depth = SWEEPS * batches
    slab = nx // slabs
    cols = ny // owners
    width = cols + 2 * depth
    rows = slab + 2 * depth
    cells = rows * width
    sources = modes // batches
    fits = (
        slab > depth
        and cells % (2 * LANES) == 0
        and (slab * cols) % LANES == 0
        and (width * depth) % LANES == 0
        and width <= LANES
        and modes == 8 * owners
        and owners == 8
        and batches == 4
        and sources == 16
        and slab % 8 == 0
        and ny == 2 * LANES
        and fields <= 28
        and fields % 2 == 0
        and batches * nz <= LANES
    )
    return fits, (batches, sources, modes, width, depth, cells, rows, fields, nz, owners, slabs)


def by_patch(dims, forcing, mean_field, coef_fields, color, pair_src, pair_field, pair_value):
    batches, sources, modes, width, depth, cells, rows, fields, nz, owners, slabs = dims
    mode_dev, slab, ny = forcing.shape
    per_batch = mode_dev // batches
    cols = ny // owners
    core_cells = slab * width
    kpad = 32
    spread = -(-(fields * sources) // LANES) * LANES

    hbm = pl.BlockSpec(memory_space=pltpu.HBM)
    f32, i32 = jnp.float32, jnp.int32
    flat = pltpu.VMEM((mode_dev * slab * ny // LANES, LANES), f32)
    vmem = pl.BlockSpec(memory_space=pltpu.VMEM)
    sems = pltpu.SemaphoreType.DMA
    got = pl.pallas_call(
        functools.partial(sweep_kernel, dims),
        out_shape=(flat, flat),
        in_specs=[hbm] * 7,
        out_specs=(vmem, vmem),
        scratch_shapes=[
            pltpu.VMEM((3, LANES, LANES), f32),
            pltpu.SMEM((modes,), i32),
            pltpu.VMEM((batches, mode_dev, nz), i32),
            pltpu.VMEM((batches, mode_dev, nz), i32),
            pltpu.VMEM((batches, mode_dev, nz), f32),
            pltpu.VMEM((mode_dev * slab, ny), f32),
            pltpu.VMEM((slab, ny), f32),
            pltpu.VMEM((ny // LANES, kpad * slab, LANES), f32),
            pltpu.VMEM((batches // 2, batches, per_batch, LANES), f32),
            pltpu.VMEM((batches // 2, owners, batches, per_batch, LANES), f32),
            pltpu.VMEM((owners, batches, per_batch, core_cells), f32),
            pltpu.VMEM((batches, owners, per_batch, cells), f32),
            pltpu.VMEM((kpad, cells), f32),
            pltpu.VMEM((4, kpad, cells), f32),
            pltpu.VMEM((1, cells), f32),
            pltpu.VMEM((batches, 2 * modes, spread), jnp.bfloat16),
            pltpu.VMEM((modes, cells), f32),
            pltpu.VMEM((modes, core_cells), f32),
            pltpu.VMEM((sources, cells + 2 * LANES), f32),
            pltpu.VMEM((2, 4, sources, cells), f32),
            pltpu.VMEM((batches, owners, per_batch, slab * cols), f32),
            pltpu.VMEM((PIECES, owners, batches, per_batch, slab * cols // PIECES), f32),
            pltpu.VMEM((batches, owners, per_batch, slab * cols), f32),
            pltpu.VMEM((PIECES, owners, batches, per_batch, slab * cols // PIECES), f32),
            sems((8,)),
            sems((4,)),
            sems((batches // 2 + 2 * batches + PIECES,)),
            sems((2,)),
            sems((2, batches)),
            sems((2,)),
            sems((2,)),
        ],
        compiler_params=pltpu.CompilerParams(
            collective_id=0, has_side_effects=True
        ),
        name="sweeps",
    )(
        color, pair_src, pair_field, pair_value, forcing.reshape(mode_dev * slab, ny), mean_field,
        coef_fields.reshape(fields * slab, ny),
    )
    plain = jax.ShapeDtypeStruct((mode_dev * slab * ny // LANES, LANES), f32)
    got = pl.pallas_call(
        leave_kernel,
        out_shape=(plain, plain),
        in_specs=[pl.BlockSpec(memory_space=pltpu.VMEM)] * 2,
        out_specs=(pl.BlockSpec(memory_space=pl.ANY),) * 2,
        scratch_shapes=[sems((2,))],
        compiler_params=pltpu.CompilerParams(vmem_limit_bytes=4_000_000),
        name="leave",
    )(*got)
    shape = (mode_dev * slab // 8, ny // LANES, 8, LANES)
    return tuple(
        x.reshape(shape).transpose(0, 2, 1, 3).reshape(mode_dev, slab, ny) for x in got
    )


def solution(mesh):
    specs = (
        P("mode", "space", None),
        P("space", None),
        P(None, "space", None),
        P(),
        P(None, "mode", None),
        P(None, "mode", None),
        P(None, "mode", None),
    )

    def whole(*args):
        fits, dims = patch_sizes(mesh, args[0], args[4], args[2])
        body = functools.partial(by_patch, dims) if fits else by_batch
        return jax.shard_map(
            body,
            mesh=mesh,
            in_specs=specs,
            out_specs=(P("mode", "space", None), P("mode", "space", None)),
            check_vma=False,
        )(*args)

    return whole
```
